32 devices in a mesh: line: 8 (over y, x, core), surf: 4 (over z).
Axes of the slice: x: 2, y: 2, z: 4, core: 2. Of those that a mesh axis runs over, the one named last changes fastest.
Arguments:
- right_side: float32 [8, 64, 135], P('surf', 'line'), may hold values from -6 to 6
- previous: float32 [8, 64, 135], P('surf', 'line'), may hold values from -6 to 6
- coupling: float32 [8, 64, 4, 135], P('surf', 'line'), may hold values from 0.1 to 0.4
- neighbours: int32 [8, 4], P('surf'), may hold values from 0 to 7, as said below
- pivots: bfloat16 [8, 64, 135, 135], P('surf', 'line'), may hold values from -0.0625 to 0.0625
- lower_factor: bfloat16 [8, 64, 135, 135], P('surf', 'line')
- upper_factor: bfloat16 [8, 64, 135, 135], P('surf', 'line')
Outputs:
- correction: float32 [8, 64, 135], P('surf', 'line')
The draws below stay inside these ranges and needn't reach their ends.
Inputs may be any that keep to these rules, and one draw needn't show every extreme that they name: `neighbours`: lines of surface patch q are q * 2 to (q + 1) * 2 - 1. Face 0 of a line in patch q names a line of patch q - 1 and face 1 one of patch q + 1 (patches wrap around); faces 2 and 3 name lines of its own patch.
All inputs are finite; a program needn't handle non-finite values.
Results may differ from the reference program's by a relative error of at most 0.0003.
Values sent between devices are 32-bit elements; how exact they have to be, the bound alone decides.
No kernel may reach another device: no remote copies, remote signals or barrier semaphores. Data moves between devices by JAX's collectives and lax.ppermute only.
A program may use at most 64 MiB of HBM per device.

```python
import math
import jax
import jax.numpy as jnp
from jax import lax

UNKNOWNS = 135
FACES = 4
LINE_DEV = 2
CELLS_PER_COLUMN = 64
COLUMN_COUNT = 8


def decay_blocks(key):
    stochastic_seeds = jax.random.split(key, 7)
    share = 0.5
    slowly = jax.random.bernoulli(stochastic_seeds[0], share, (COLUMN_COUNT, 1, UNKNOWNS))
    slow_rate = jnp.exp(jax.random.uniform(stochastic_seeds[1], (COLUMN_COUNT, 1, UNKNOWNS), jnp.float32, math.log(0.6), math.log(1.2))) / CELLS_PER_COLUMN
    fast_rate = jnp.exp(jax.random.uniform(stochastic_seeds[2], (COLUMN_COUNT, 1, UNKNOWNS), jnp.float32, math.log(1.0 / 50.0), math.log(1.0 / 30.0)))
    base_rate = jnp.where(slowly, slow_rate, fast_rate)
    varied = jnp.exp(jax.random.uniform(stochastic_seeds[3], (COLUMN_COUNT, CELLS_PER_COLUMN, 1), jnp.float32, math.log(0.7), math.log(1.5)))
    places = jax.random.randint(stochastic_seeds[4], (COLUMN_COUNT, 3), 0, CELLS_PER_COLUMN)
    deleted_equations = jnp.any(jnp.arange(CELLS_PER_COLUMN)[None, :, None] == places[:, None, :], axis=-1)
    correction_group = jax.random.uniform(stochastic_seeds[5], (COLUMN_COUNT, CELLS_PER_COLUMN, 1), jnp.float32, 0.5, 0.8)
    submatrix_multiplier = jnp.where(deleted_equations[:, :, None], correction_group, 1.0)
    diagonal = jnp.exp(-base_rate * varied) * submatrix_multiplier
    spread = 0.15 / math.sqrt(UNKNOWNS)
    noise = jax.random.normal(stochastic_seeds[6], (COLUMN_COUNT, CELLS_PER_COLUMN, UNKNOWNS, UNKNOWNS), jnp.float32) * spread
    identity = jnp.eye(UNKNOWNS, dtype=jnp.float32)
    noise = noise * (1.0 - identity)
    scaled = diagonal[:, :, :, None] * (identity + noise) / math.sqrt(1.0 + (UNKNOWNS - 1) * spread * spread)
    return scaled.astype(jnp.bfloat16)


def draw_lower_factor(key, part):
    return decay_blocks(jax.random.fold_in(key, 11))


def draw_upper_factor(key, part):
    return decay_blocks(jax.random.fold_in(key, 12))


def draw_neighbours(key, part):
    stochastic_seeds = jax.random.split(jax.random.fold_in(key, 13), 2)
    patches = COLUMN_COUNT // LINE_DEV
    line_ids = jnp.arange(COLUMN_COUNT, dtype=jnp.int32)
    patch = line_ids // LINE_DEV
    within = line_ids % LINE_DEV
    offsets = jax.random.randint(stochastic_seeds[0], (patches, 2), 0, LINE_DEV)
    before = (patch - 1 + patches) % patches * LINE_DEV + (within + offsets[patch, 0]) % LINE_DEV
    after = (patch + 1) % patches * LINE_DEV + (within + offsets[patch, 1]) % LINE_DEV
    inside = patch[:, None] * LINE_DEV + jax.random.randint(stochastic_seeds[1], (COLUMN_COUNT, 2), 0, LINE_DEV)
    return jnp.concatenate([before[:, None], after[:, None], inside], axis=1).astype(jnp.int32)


def block_scale(key, extent, cuts, smallest, top_value):
    def one(position, shards_of):
        draws = jax.random.uniform(jax.random.fold_in(jax.random.fold_in(key, 6), position), (shards_of,), jnp.float32, smallest / len(cuts), top_value / len(cuts))
        return jnp.repeat(jnp.exp(draws), extent[position] // shards_of).reshape((-1,) + (1,) * (len(extent) - position - 1))

    gain = one(*cuts[0])
    for cut in cuts[1:]:
        gain = gain * one(*cut)
    return gain


def bell_draw(key, extent, scale, limit, shards=(), kind=jnp.bfloat16):
    values = scale * jax.random.normal(key, extent, jnp.float32)
    if shards:
        values = values * block_scale(key, extent, shards, -0.22, 0.18)
    return jnp.clip(values, -limit, limit).astype(kind)


def setup_inputs(seed: int = 0) -> dict:
    splits = jax.random.split(jax.random.key(seed), 8)
    return {
        "right_side": bell_draw(splits[0], (COLUMN_COUNT, CELLS_PER_COLUMN, UNKNOWNS), 1.0, 6.0, ((0, 4), (1, 8)), jnp.float32),
        "previous": bell_draw(splits[1], (COLUMN_COUNT, CELLS_PER_COLUMN, UNKNOWNS), 1.0, 6.0, ((0, 4), (1, 8)), jnp.float32),
        "coupling": jnp.clip(0.1 + 0.3 * jax.random.uniform(splits[2], (COLUMN_COUNT, CELLS_PER_COLUMN, FACES, UNKNOWNS), jnp.float32) ** block_scale(splits[2], (COLUMN_COUNT, CELLS_PER_COLUMN, FACES, UNKNOWNS), ((0, 4), (1, 8)), -0.2, 0.2), 0.1, 0.4),
        "neighbours": draw_neighbours(jax.random.fold_in(splits[7], 71), 0),
        "pivots": bell_draw(splits[4], (COLUMN_COUNT, CELLS_PER_COLUMN, UNKNOWNS, UNKNOWNS), (UNKNOWNS * 64) ** -0.5, 0.0625, ((0, 4), (1, 8))),
        "lower_factor": draw_lower_factor(jax.random.fold_in(splits[7], 71), 0),
        "upper_factor": draw_upper_factor(jax.random.fold_in(splits[7], 71), 0),
    }


def pick_block(blocks, element):
    return lax.dynamic_index_in_dim(blocks, element, 1, keepdims=False).astype(jnp.float32)


def apply_block(matrix, vector):
    return jnp.einsum("lab,lb->la", matrix, vector, precision=lax.Precision.HIGHEST)


def reference(right_side, previous, coupling, neighbours, pivots, lower_factor, upper_factor):
    nearby = jnp.take(previous, neighbours, axis=0)
    face_sum = jnp.sum(coupling * jnp.transpose(nearby, (0, 2, 1, 3)), axis=2)
    source = right_side - face_sum

    def forward(carried, element):
        driven = apply_block(pick_block(pivots, element), lax.dynamic_index_in_dim(source, element, 1, keepdims=False))
        result = driven + apply_block(pick_block(lower_factor, element), carried)
        return result, result

    start = jnp.zeros((COLUMN_COUNT, UNKNOWNS), jnp.float32)
    _, sweep = lax.scan(forward, start, jnp.arange(CELLS_PER_COLUMN, dtype=jnp.int32))

    def backward(carried, element):
        result = sweep[element] + apply_block(pick_block(upper_factor, element), carried)
        return result, result

    _, solved = lax.scan(backward, start, jnp.arange(CELLS_PER_COLUMN, dtype=jnp.int32), reverse=True)
    return jnp.transpose(solved, (1, 0, 2))
```

```python
import functools

import jax
import jax.numpy as jnp
from jax import lax
from jax.experimental import pallas as pl
from jax.experimental.pallas import tpu as pltpu
from jax.sharding import PartitionSpec as P

F32 = jnp.float32
BF16 = jnp.bfloat16
VMEM = pl.BlockSpec(memory_space=pltpu.VMEM)
SMEM = pl.BlockSpec(memory_space=pltpu.SMEM)
LANES = 256
LIMIT = 40 * 1024 * 1024


def dot_nt(a, b):
    return lax.dot_general(a, b, (((1,), (1,)), ((), ())), preferred_element_type=F32)


def dot_nn(a, b):
    return lax.dot_general(a, b, (((1,), (0,)), ((), ())), preferred_element_type=F32)


def stacked(x):
    rest = x - x.astype(BF16).astype(F32)
    return jnp.concatenate([x, rest], axis=0).astype(BF16)


def times_block(x, block):
    n = x.shape[0]
    r = dot_nt(stacked(x), block)
    return r[:n] + r[n:]


def times_map(x, m):
    n = x.shape[0]
    hi = m.astype(BF16)
    lo = (m - hi.astype(F32)).astype(BF16)
    a = stacked(x)
    r = dot_nn(a, hi)
    return r[:n] + r[n:] + dot_nn(a[:n], lo)


def maps_kernel(lower, upper, tail, lead):
    rows, cells, width, _ = lower.shape
    high = lead.shape[1]
    eye = (
        lax.broadcasted_iota(jnp.int32, (high, width), 0)
        == lax.broadcasted_iota(jnp.int32, (high, width), 1)
    ).astype(BF16)
    lead[...] = jnp.zeros(lead.shape, F32)
    tail[...] = jnp.zeros(tail.shape, F32)
    for i in range(cells):
        for l in range(rows):
            if i == 0:
                now = dot_nt(eye, lower[l, 0])
            else:
                now = times_block(tail[l, i - 1, :high, :width], lower[l, i])
            tail[l, i, :high, :width] = now
    for l in range(rows):
        lead[l, :, :width] = tail[l, cells - 1, :high, :width]
    for i in reversed(range(cells)):
        for l in range(rows):
            if i == cells - 1:
                tail[l, i, high:, :width] = dot_nt(eye, upper[l, i])
                continue_g = dot_nt(eye, upper[l, i])
            else:
                both = times_block(tail[l, i + 1, :, :width], upper[l, i])
                tail[l, i, :high, :width] += both[:high]
                tail[l, i, high:, :width] = both[high:]


def segment_kernel(
    where, neighbours, right, own, first, second, coupling, pivots, lower, upper,
    lead, tail, inner, keep, send, near,
):
    rows, cells, width = right.shape
    high = lead.shape[1]
    core = where[0]
    here = where[1]
    patches = where[2]
    for l in range(rows):
        near[l] = own[l]
        near[rows + l] = first[l]
        near[2 * rows + l] = second[l]
    even = lax.rem(here, 2) == 0
    driven = []
    for l in range(rows):
        total = right[l]
        for f in range(coupling.shape[2]):
            line = neighbours[l, f]
            patch = line // rows
            ahead = lax.rem(patch - here + patches, patches)
            before = jnp.where(even, 2, 1)
            after = jnp.where(even, 1, 2)
            slot = jnp.where(ahead == 0, 0, jnp.where(ahead == 1, after, before))
            total = total - coupling[l, :, f, :] * near[slot * rows + lax.rem(line, rows)]
        driven.append(total)
    lhs = [stacked(d) for d in driven]
    value = [None] * rows
    values = [[None] * cells for _ in range(rows)]
    for i in range(cells):
        for l in range(rows):
            r = dot_nt(lhs[l], pivots[l, i])
            d = jnp.broadcast_to(r[i : i + 1] + r[cells + i : cells + i + 1], (8, width))
            if i:
                d = d + times_block(value[l], lower[l, i])
            value[l] = d
            values[l][i] = d
    corr = [None] * rows
    for i in reversed(range(cells)):
        for l in range(rows):
            d = values[l][i]
            if i < cells - 1:
                d = d + times_block(corr[l], upper[l, i])
            corr[l] = d
            inner[l, i : i + 1, :] = d[:1]
    unit = (lax.broadcasted_iota(jnp.int32, (high, LANES), 0) == high - 1) & (
        lax.broadcasted_iota(jnp.int32, (high, LANES), 1) == high - 1
    )
    for l in range(rows):
        def put(dst):
            dst[0] = jnp.where(unit, 1.0, lead[l])
            dst[1] = tail[l, 0, :high, :]
            dst[2] = tail[l, 0, high:, :]
            dst[0, width : width + 1, :width] = value[l][:1]
            dst[1, width : width + 1, :width] = corr[l][:1]

        @pl.when(core == l)
        def _():
            put(keep)

        @pl.when(core != l)
        def _():
            put(send)


def merge_kernel(side, mine, theirs, down, up):
    s = side[0]
    high = mine.shape[1]

    def pick(k):
        a, b = mine[k], theirs[k]
        return jnp.where(s == 0, a, b), jnp.where(s == 0, b, a)

    f_left, f_right = pick(0)
    g_left, g_right = pick(1)
    b_left, b_right = pick(2)
    down[0] = f_left
    down[1] = g_right
    down[2] = b_right
    lhs = f_left[:, :high]
    up[0] = times_map(lhs, f_right)
    inner = times_map(lhs, g_right)
    both = times_map(jnp.concatenate([inner, b_right], axis=0)[:, :high], b_left)
    up[1] = g_left + both[:high]
    up[2] = both[high:]


def top_kernel(sides, mine, theirs, *refs):
    downs, out = refs[:-1], refs[-1]
    levels = len(downs)
    s = sides[levels]
    high = mine.shape[1]
    f_left = jnp.where(s == 0, mine[0], theirs[0])
    g_right = jnp.where(s == 0, theirs[1], mine[1])
    unit = lax.broadcasted_iota(jnp.int32, (8, LANES), 1) == high - 1
    one = jnp.where(unit, 1.0, 0.0)
    middle = jnp.broadcast_to(f_left[high - 1 : high], (8, LANES))
    back = times_map(middle[:, :high], g_right)
    value = jnp.where(s == 0, one, middle)
    corr = jnp.where(s == 0, back, 0.0)
    for k in reversed(range(levels)):
        d = downs[k]
        middle = times_map(value[:, :high], d[0])
        back = times_map(middle[:, :high], d[1]) + times_map(corr[:, :high], d[2])
        if k:
            value = jnp.where(sides[k] == 0, value, middle)
            corr = jnp.where(sides[k] == 0, back, corr)
        else:
            out[0] = jnp.where(sides[0] == 0, value, middle)
            out[1] = jnp.where(sides[0] == 0, back, corr)
            out[2] = jnp.where(sides[0] == 0, middle, value)
            out[3] = jnp.where(sides[0] == 0, corr, back)


def final_kernel(where, mine, theirs, inner, tail, out):
    rows, cells, width = inner.shape
    high = tail.shape[2] // 2
    core = where[0]
    for l in range(rows):
        y = jnp.where(core == l, mine[0], theirs[0])
        c = jnp.where(core == l, mine[1], theirs[1])
        ycol = jnp.transpose(y)[:high, :1]
        ccol = jnp.transpose(c)[:high, :1]
        for i in range(cells):
            t = tail[l, i, :high, :] * ycol + tail[l, i, high:, :] * ccol
            out[l, i : i + 1, :] = inner[l, i : i + 1, :] + jnp.sum(t, axis=0, keepdims=True)[:, :width]


def call(body, outs, specs, scratch=()):
    return pl.pallas_call(
        body,
        out_shape=outs,
        in_specs=specs,
        out_specs=jax.tree.map(lambda _: VMEM, outs),
        scratch_shapes=scratch,
        compiler_params=pltpu.CompilerParams(vmem_limit_bytes=LIMIT),
    )


def f32(*shape):
    return jax.ShapeDtypeStruct(shape, F32)


def shards(right_side, previous, coupling, neighbours, pivots, lower_factor, upper_factor):
    rows, cells, width = right_side.shape
    high = width + 1
    patches = lax.axis_size("surf")
    here = lax.axis_index("surf")
    count = lax.axis_size("line")
    place = lax.axis_index("line")
    levels = count.bit_length() - 1
    core = place % 2
    pairs = [(i, i + 1 - 2 * (i % 2)) for i in range(patches)]
    odd = [(i, (i - 1 + 2 * (i % 2)) % patches) for i in range(patches)]
    second = lax.ppermute(previous, "surf", odd)
    first = lax.ppermute(previous, "surf", pairs)
    where = jnp.stack([core, here, jnp.int32(patches)]).astype(jnp.int32)
    sides = jnp.stack([(place >> k) & 1 for k in range(levels)]).astype(jnp.int32)
    tail, lead = call(
        maps_kernel,
        [f32(rows, cells, 2 * high, LANES), f32(rows, high, LANES)],
        [VMEM] * 2,
    )(lower_factor, upper_factor)
    inner, keep, send = call(
        segment_kernel,
        [f32(rows, cells, width), f32(3, high, LANES), f32(3, high, LANES)],
        [SMEM] * 2 + [VMEM] * 10,
        [pltpu.VMEM((3 * rows, cells, width), F32)],
    )(
        where, neighbours, right_side, previous, first, second, coupling, pivots,
        lower_factor, upper_factor, lead, tail,
    )
    swap = lambda a, k: lax.ppermute(a, "line", [(i, i ^ (1 << k)) for i in range(count)])
    downs = []
    theirs = swap(send, 0)
    mine = keep
    for k in range(levels - 1):
        down, mine = call(
            merge_kernel, [f32(3, high, LANES), f32(3, high, LANES)], [SMEM, VMEM, VMEM]
        )(sides[k : k + 1], mine, theirs)
        downs.append(down)
        if k + 1 == levels - 1:
            mine = mine[:2]
        theirs = swap(mine, k + 1)
    ends = call(top_kernel, [f32(4, 8, LANES)], [SMEM] + [VMEM] * (2 + len(downs)))(
        sides, mine, theirs, *downs
    )[0]
    other = swap(ends[2:], 0)
    return call(final_kernel, [f32(rows, cells, width)], [SMEM] + [VMEM] * 4)(
        where, ends[:2], other, inner, tail
    )[0]


def solution(mesh):
    return jax.shard_map(
        shards,
        mesh=mesh,
        in_specs=(
            P("surf", "line", None),
            P("surf", "line", None),
            P("surf", "line", None, None),
            P("surf", None),
            P("surf", "line", None, None),
            P("surf", "line", None, None),
            P("surf", "line", None, None),
        ),
        out_specs=P("surf", "line", None),
        check_vma=False,
    )
```

```python
import functools

import jax
import jax.numpy as jnp
from jax import lax
from jax.experimental import pallas as pl
from jax.experimental.pallas import tpu as pltpu
from jax.sharding import PartitionSpec as P

F32 = jnp.float32
BF16 = jnp.bfloat16
VMEM = pl.BlockSpec(memory_space=pltpu.VMEM)
LANES = 256
LIMIT = 12 * 1024 * 1024


def dot_nt(a, b):
    return lax.dot_general(a, b, (((1,), (1,)), ((), ())), preferred_element_type=F32)


def dot_nn(a, b):
    return lax.dot_general(a, b, (((1,), (0,)), ((), ())), preferred_element_type=F32)


def stacked(x):
    rest = x - x.astype(BF16).astype(F32)
    return jnp.concatenate([x, rest], axis=0).astype(BF16)


def times_block(x, block):
    n = x.shape[0]
    r = dot_nt(stacked(x), block)
    return r[:n] + r[n:]


def times_map(x, m):
    n = x.shape[0]
    hi = m.astype(BF16)
    lo = (m - hi.astype(F32)).astype(BF16)
    a = stacked(x)
    r = dot_nn(a, hi)
    return r[:n] + r[n:] + dot_nn(a[:n], lo)


def vector(row):
    return jnp.broadcast_to(row, (8, row.shape[1]))


def packed(m):
    top = jnp.transpose(m[:128, 128:])[:8]
    return jnp.concatenate([m[:, :128], top, m[128:, 128:]], axis=0)


def unpacked(p):
    high = p.shape[0] - 16
    top = jnp.concatenate([p[high : high + 8], jnp.zeros((120, 128), F32)], axis=0)
    right = jnp.concatenate([jnp.transpose(top), p[high + 8 :]], axis=0)
    return jnp.concatenate([p[:high], right], axis=1)


def maps_kernel(lower, upper, tail, half, keep, send):
    rows, cells, width, _ = lower.shape
    high = keep.shape[1]
    per = cells // 2
    core = side(0)
    eye = (
        lax.broadcasted_iota(jnp.int32, (high, width), 0)
        == lax.broadcasted_iota(jnp.int32, (high, width), 1)
    ).astype(BF16)
    blank = jnp.zeros((high, LANES - 128), F32)
    for k in range(3):
        keep[k, :, 128:] = blank
        send[k, :, 128:] = blank
        for l in range(rows):
            half[l, k, :, 128:] = blank
    chains = [(l, p) for l in range(rows) for p in range(2)]
    ahead = {}
    for j in range(per):
        for l, p in chains:
            i = p * per + j
            block = lower[l, i]
            ahead[l, p] = times_block(ahead[l, p], block) if j else dot_nt(eye, block)
            tail[l, i, :high, :width] = ahead[l, p]
    back = {}
    for j in reversed(range(per)):
        for l, p in chains:
            i = p * per + j
            if j == per - 1:
                back[l, p] = jnp.concatenate([ahead[l, p], dot_nt(eye, upper[l, i])], axis=0)
            else:
                both = times_block(back[l, p], upper[l, i])
                front = tail[l, i, :high, :width] + both[:high]
                back[l, p] = jnp.concatenate([front, both[high:]], axis=0)
                tail[l, i, :high, :width] = front
            tail[l, i, high:, :width] = back[l, p][high:]
    joint = []
    for l in range(rows):
        f = ahead[l, 0], ahead[l, 1]
        g = back[l, 0][:high], back[l, 1][:high]
        b = back[l, 0][high:], back[l, 1][high:]
        inward = times_map(f[0], g[1][:width])
        both = times_map(jnp.concatenate([inward, b[1]], axis=0), b[0][:width])
        for k, m in enumerate([f[0], inward, f[1]]):
            half[l, k, :, :width] = m
        joint.append([times_map(f[0], f[1][:width]), g[0] + both[:high], both[high:]])
    for k in range(3):
        keep[k, :, :width] = jnp.where(core == 0, joint[0][k], joint[1][k])
        send[k, :, :width] = jnp.where(core == 0, joint[1][k], joint[0][k])


def segment_kernel(
    patches, neighbours, right, own, first, second, coupling, pivots, lower, upper,
    tail, half, inner, bias, keep, send, pad,
):
    rows, cells, width = right.shape
    high = half.shape[2]
    per = cells // 2
    core = side(0)
    here = lax.axis_index("surf")
    odd = lax.rem(here, 2)
    after = lax.rem(here + 1, patches)
    before = lax.rem(here + patches - 1, patches)
    met = [here, jnp.where(odd == 0, after, before), jnp.where(odd == 0, before, after)]
    driven = []
    for l in range(rows):
        total = right[l]
        for f in range(coupling.shape[2]):
            line = jnp.broadcast_to(neighbours[l : l + 1, f : f + 1], (cells, width))
            near = jnp.zeros((cells, width), F32)
            for patch, held in zip(met, (own, first, second)):
                for r in range(rows):
                    near = jnp.where(line == patch * rows + r, held[r], near)
            total = total - coupling[l, :, f, :] * near
        driven.append(total)
    lhs = [stacked(d) for d in driven]
    chains = [(l, p) for l in range(rows) for p in range(2)]
    value, values, corr = {}, {}, {}
    for j in range(per):
        for l, p in chains:
            i = p * per + j
            r = dot_nt(lhs[l], pivots[l, i])
            d = vector(r[i : i + 1] + r[cells + i : cells + i + 1])
            if j:
                d = d + times_block(value[l, p], lower[l, i])
            value[l, p] = values[l, i] = d
    for j in reversed(range(per)):
        for l, p in chains:
            i = p * per + j
            d = values[l, i]
            if j < per - 1:
                d = d + times_block(corr[l, p], upper[l, i])
            corr[l, p] = d
            inner[l, i : i + 1, :] = d[:1]
    pad[...] = jnp.zeros(pad.shape, F32)
    ends = []
    for l in range(rows):
        for p in range(2):
            pad[l, p, :, :width] = value[l, p]
            pad[l, 2 + p, :, :width] = corr[l, p]
        f = [pad[l, 0], pad[l, 1]]
        g = [pad[l, 2], pad[l, 3]]
        v = merged_vectors(f, g, half[l, 2], tail[l, per, :high], tail[l, 0, high:])
        bias[l, 0] = f[0]
        bias[l, 1] = v[2]
        ends.append(v)
    keep[...] = jnp.zeros(keep.shape, F32)
    send[...] = jnp.zeros(send.shape, F32)
    for k in range(2):
        a, b = ends[0][k][:1, :width], ends[1][k][:1, :width]
        keep[k : k + 1, :width] = jnp.where(core == 0, a, b)
        send[k : k + 1, :width] = jnp.where(core == 0, b, a)


def side(level):
    return (lax.axis_index("line") >> level) & 1


def ordered(s, mine, theirs):
    return jnp.where(s == 0, mine, theirs), jnp.where(s == 0, theirs, mine)


def merged_maps(f, g, b, lean):
    high = f[0].shape[0]
    lhs = f[0][:, :high]
    inward = times_map(lhs, g[1])
    if lean:
        return [g[0] + times_map(inward[:, :high], b[0])], inward
    both = times_map(jnp.concatenate([inward, b[1]], axis=0)[:, :high], b[0])
    return [times_map(lhs, f[1]), g[0] + both[:high], both[high:]], inward


def merged_vectors(f, g, f_right, g_right, b_left):
    high = f_right.shape[0]
    between = times_map(f[0][:, :high], g_right) + g[1]
    return times_map(f[0][:, :high], f_right) + f[1], g[0] + times_map(between[:, :high], b_left), between


def first_maps_kernel(mine, theirs, after, down, full, pack):
    s = side(0)
    f, g, b = (ordered(s, mine[k], theirs[k]) for k in range(3))
    joint, inward = merged_maps(f, g, b, False)
    for k, m in enumerate([f[0], inward, b[1], f[1], g[1], b[0]]):
        down[k] = m
    size = pack.shape[0] // len(joint)
    for k, m in enumerate(joint):
        full[k] = m
        pack[k * size : (k + 1) * size] = packed(m)


def first_vectors_kernel(down, mine, theirs, out, bias):
    s = side(0)
    f = [vector(v) for v in ordered(s, mine[0:1], theirs[0:1])]
    g = [vector(v) for v in ordered(s, mine[1:2], theirs[1:2])]
    joint = merged_vectors(f, g, down[3], down[4], down[5])
    out[...] = jnp.zeros(out.shape, F32)
    out[0:1] = joint[0][:1]
    out[1:2] = joint[1][:1]
    bias[0] = f[0]
    bias[1] = joint[2]


def level_kernel(level, split, lean, mine, theirs, vectors, others, down, full, bias, out):
    high = mine.shape[1]
    size = high + 16
    maps = [unpacked(theirs[k * size : (k + 1) * size]) for k in range(3)]
    s = side(level)
    f, g, b = (ordered(s, mine[k], maps[k]) for k in range(3))
    joint, inward = merged_maps(f, g, b, lean)
    for k, m in enumerate([f[0], inward, b[1]]):
        down[k] = m
    if split:
        other = [others[0:1], others[1:2]]
    else:
        other = tail_vectors(theirs, 3 * size)
    vf = [vector(v) for v in ordered(s, vectors[0:1], other[0])]
    vg = [vector(v) for v in ordered(s, vectors[1:2], other[1])]
    v = merged_vectors(vf, vg, f[1], g[1], b[0])
    bias[0] = vf[0]
    bias[1] = v[2]
    for k, m in enumerate(joint):
        out[k * size : (k + 1) * size] = packed(m)
        if not lean:
            full[k] = m
    base = len(joint) * size
    full_vectors = jnp.concatenate([v[0][:1], v[1][:1]], axis=0)
    out[base : base + 2] = full_vectors[:, :128]
    out[base + 2 : base + 4] = full_vectors[:, 128:]
    out[base + 4 : base + 8] = jnp.zeros((4, 128), F32)
    full[full.shape[0] - 1, 0:2] = full_vectors


def tail_vectors(theirs, base):
    return [
        jnp.concatenate([theirs[base + k : base + k + 1], theirs[base + 2 + k : base + 3 + k]], axis=1)
        for k in range(2)
    ]


def top_kernel(levels, *refs):
    sides = [side(k) for k in range(levels + 1)]
    mine, theirs = refs[:2]
    downs, biases = refs[2 : levels + 2], refs[levels + 2 : 2 * levels + 2]
    keep, send = refs[-2:]
    s = sides[levels]
    size = theirs.shape[0] - 8
    high = size - 16
    g = unpacked(theirs[:size])
    other = [vector(v) for v in tail_vectors(theirs, size)]
    ours = vector(mine[mine.shape[0] - 1, 0:1])
    back = times_map(ours[:, :high], g) + other[1]
    value = jnp.where(s == 0, 0.0, other[0])
    corr = jnp.where(s == 0, back, 0.0)
    for k in reversed(range(levels)):
        d = downs[k]
        lhs = value[:, :high]
        middle = times_map(lhs, d[0]) + biases[k][0]
        back = times_map(lhs, d[1]) + times_map(corr[:, :high], d[2]) + biases[k][1]
        if k:
            value = jnp.where(sides[k] == 0, value, middle)
            corr = jnp.where(sides[k] == 0, back, corr)
    left = sides[0] == 0
    keep[0] = jnp.where(left, value, middle)
    keep[1] = jnp.where(left, back, corr)
    send[0] = jnp.where(left, middle, value)
    send[1] = jnp.where(left, corr, back)


def final_kernel(mine, theirs, inner, tail, half, bias, out):
    rows, cells, width = inner.shape
    high = half.shape[2]
    per = cells // 2
    core = side(0)
    index = lax.broadcasted_iota(jnp.int32, (8, LANES), 0)
    gathered = jnp.zeros((8, LANES), F32)
    for l in range(rows):
        y = jnp.where(core == l, mine[0], theirs[0])
        c = jnp.where(core == l, mine[1], theirs[1])
        lhs = y[:, :high]
        middle = times_map(lhs, half[l, 0]) + bias[l, 0]
        between = (
            times_map(lhs, half[l, 1])
            + times_map(c[:, :high], tail[l, per, high:])
            + bias[l, 1]
        )
        for k, v in enumerate([y, between, middle, c]):
            gathered = jnp.where(index == 4 * l + k, v, gathered)
    columns = jnp.transpose(gathered)[:high]
    for l in range(rows):
        for p in range(2):
            k = 4 * l + 2 * p
            ycol = jnp.broadcast_to(columns[:, k : k + 1], (high, 128))
            ccol = jnp.broadcast_to(columns[:, k + 1 : k + 2], (high, 128))
            col = jnp.concatenate([ycol, ccol], axis=0)
            for i in range(p * per, p * per + per):
                for h in range(2):
                    at = slice(128 * h, min(width, 128 * h + 128))
                    t = tail[l, i, :, 128 * h : 128 * h + 128] * col
                    r = jnp.sum(t, axis=0, keepdims=True)
                    out[l, i : i + 1, at] = inner[l, i : i + 1, at] + r[:, : at.stop - at.start]


def call(body, outs, specs, scratch=()):
    return pl.pallas_call(
        body,
        out_shape=outs,
        in_specs=specs,
        out_specs=jax.tree.map(lambda _: VMEM, outs),
        scratch_shapes=scratch,
        compiler_params=pltpu.CompilerParams(vmem_limit_bytes=LIMIT),
    )


def f32(*shape):
    return jax.ShapeDtypeStruct(shape, F32)


def shards(right_side, previous, coupling, neighbours, pivots, lower_factor, upper_factor):
    rows, cells, width = right_side.shape
    high = width + 1
    size = high + 16
    patches = lax.axis_size("surf")
    count = lax.axis_size("line")
    levels = count.bit_length() - 1
    pairs = [(i, i + 1 - 2 * (i % 2)) for i in range(patches)]
    odd = [(i, (i - 1 + 2 * (i % 2)) % patches) for i in range(patches)]
    swap = lambda a, k: lax.ppermute(a, "line", [(i, i ^ (1 << k)) for i in range(count)])
    second = lax.ppermute(previous, "surf", odd)
    first = lax.ppermute(previous, "surf", pairs)
    full = f32(3, high, LANES)
    row = f32(8, LANES)
    tail, half, keep, send = call(
        maps_kernel,
        [f32(rows, cells, 2 * high, LANES), f32(rows, 3, high, LANES), full, full],
        [VMEM] * 2,
    )(lower_factor, upper_factor)
    theirs = swap(send, 0)
    inner, ends, vkeep, vsend = call(
        functools.partial(segment_kernel, patches),
        [f32(rows, cells, width), f32(rows, 2, 8, LANES), row, row],
        [VMEM] * 11,
        [pltpu.VMEM((rows, 4, 8, LANES), F32)],
    )(
        neighbours, right_side, previous, first, second, coupling, pivots,
        lower_factor, upper_factor, tail, half,
    )
    down, mine, pack = call(
        first_maps_kernel,
        [f32(6, high, LANES), full, f32(3 * size, 128)],
        [VMEM] * 3,
    )(keep, theirs, vkeep)
    theirs = swap(pack, 1)
    vtheirs = swap(vsend, 0)
    vectors, bias = call(
        first_vectors_kernel, [row, f32(2, 8, LANES)], [VMEM] * 3
    )(down, vkeep, vtheirs)
    others = swap(vectors, 1)
    downs = [down]
    biases = [bias]
    for k in range(1, levels - 1):
        lean = k == levels - 2
        down, mine, bias, pack = call(
            functools.partial(level_kernel, k, k == 1, lean),
            [
                full, f32(1 if lean else 4, high, LANES), f32(2, 8, LANES),
                f32((1 if lean else 3) * size + 8, 128),
            ],
            [VMEM] * 4,
        )(mine, theirs, vectors, others)
        downs.append(down)
        biases.append(bias)
        vectors = others = mine[-1, :8]
        theirs = swap(pack, k + 1)
    keep, send = call(
        functools.partial(top_kernel, levels - 1),
        [f32(2, 8, LANES)] * 2,
        [VMEM] * (2 + 2 * len(downs)),
    )(mine, theirs, *downs, *biases)
    return call(final_kernel, [f32(rows, cells, width)], [VMEM] * 6)(
        keep, swap(send, 0), inner, tail, half, ends
    )[0]


def solution(mesh):
    return jax.shard_map(
        shards,
        mesh=mesh,
        in_specs=(
            P("surf", "line", None),
            P("surf", "line", None),
            P("surf", "line", None, None),
            P("surf", None),
            P("surf", "line", None, None),
            P("surf", "line", None, None),
            P("surf", "line", None, None),
        ),
        out_specs=P("surf", "line", None),
        check_vma=False,
    )
```

```python
import functools

import jax
import jax.numpy as jnp
from jax import lax
from jax.experimental import pallas as pl
from jax.experimental.pallas import tpu as pltpu
from jax.sharding import PartitionSpec as P

F32 = jnp.float32
BF16 = jnp.bfloat16
VMEM = pl.BlockSpec(memory_space=pltpu.VMEM)
LANES = 256
LIMIT = 12 * 1024 * 1024


def dot_nt(a, b):
    return lax.dot_general(a, b, (((1,), (1,)), ((), ())), preferred_element_type=F32)


def dot_nn(a, b):
    return lax.dot_general(a, b, (((1,), (0,)), ((), ())), preferred_element_type=F32)


def stacked(x):
    rest = x - x.astype(BF16).astype(F32)
    return jnp.concatenate([x, rest], axis=0).astype(BF16)


def times_block(x, block):
    n = x.shape[0]
    r = dot_nt(stacked(x), block)
    return r[:n] + r[n:]


def times_map(x, m):
    n = x.shape[0]
    hi = m.astype(BF16)
    lo = (m - hi.astype(F32)).astype(BF16)
    a = stacked(x)
    r = dot_nn(a, hi)
    return r[:n] + r[n:] + dot_nn(a[:n], lo)


def vector(row):
    return jnp.broadcast_to(row, (8, row.shape[1]))


def packed(m):
    top = jnp.transpose(m[:128, 128:])[:8]
    return jnp.concatenate([m[:, :128], top, m[128:, 128:]], axis=0)


def unpacked(p):
    high = p.shape[0] - 16
    top = jnp.concatenate([p[high : high + 8], jnp.zeros((120, 128), F32)], axis=0)
    right = jnp.concatenate([jnp.transpose(top), p[high + 8 :]], axis=0)
    return jnp.concatenate([p[:high], right], axis=1)


def unit_kernel(out):
    out[...] = (
        lax.broadcasted_iota(jnp.int32, out.shape, 0) == lax.broadcasted_iota(jnp.int32, out.shape, 1)
    ).astype(BF16)


def ahead_kernel(unit, lower, ahead):
    rows, cells, width, _ = lower.shape
    per = cells // 2
    eye = unit[...]
    now = {}
    for j in range(per):
        for l in range(rows):
            for p in range(2):
                block = lower[l, p * per + j]
                if j > 1:
                    now[l, p] = times_block(now[l, p], block)
                else:
                    now[l, p] = dot_nt(now[l, p].astype(BF16) if j else eye, block)
                ahead[l, p * per + j, :, :width] = now[l, p]


def maps_kernel(unit, ahead, upper, tail, half, keep, send):
    rows, cells, width, _ = upper.shape
    high = keep.shape[1]
    per = cells // 2
    core = side(0)
    eye = unit[...]
    blank = jnp.zeros((high, LANES - 128), F32)
    for k in range(3):
        keep[k, :, 128:] = blank
        send[k, :, 128:] = blank
        for l in range(rows):
            half[l, k, :, 128:] = blank
    back = {}
    for j in reversed(range(per)):
        for l in range(rows):
            for p in range(2):
                i = p * per + j
                if j == per - 1:
                    now = jnp.concatenate(
                        [ahead[l, i, :, :width], dot_nt(eye, upper[l, i])], axis=0
                    )
                else:
                    both = times_block(back[l, p], upper[l, i])
                    now = jnp.concatenate(
                        [ahead[l, i, :, :width] + both[:high], both[high:]], axis=0
                    )
                back[l, p] = now
                tail[l, i, :, :width] = now
    joint = []
    for l in range(rows):
        f = [ahead[l, p * per + per - 1, :, :width] for p in range(2)]
        g = back[l, 0][:high], back[l, 1][:high]
        b = back[l, 0][high:], back[l, 1][high:]
        inward = times_map(f[0], g[1][:width])
        both = times_map(jnp.concatenate([inward, b[1]], axis=0), b[0][:width])
        for k, m in enumerate([f[0], inward, f[1]]):
            half[l, k, :, :width] = m
        joint.append([times_map(f[0], f[1][:width]), g[0] + both[:high], both[high:]])
    for k in range(3):
        keep[k, :, :width] = jnp.where(core == 0, joint[0][k], joint[1][k])
        send[k, :, :width] = jnp.where(core == 0, joint[1][k], joint[0][k])


def segment_kernel(
    patches, neighbours, right, own, first, second, coupling, pivots, lower, upper,
    tail, half, after, inner, bias, keep, send, pad,
):
    rows, cells, width = right.shape
    high = half.shape[2]
    per = cells // 2
    core = side(0)
    here = lax.axis_index("surf")
    odd = lax.rem(here, 2)
    after = lax.rem(here + 1, patches)
    before = lax.rem(here + patches - 1, patches)
    met = [here, jnp.where(odd == 0, after, before), jnp.where(odd == 0, before, after)]
    driven = []
    for l in range(rows):
        total = right[l]
        for f in range(coupling.shape[2]):
            line = jnp.broadcast_to(neighbours[l : l + 1, f : f + 1], (cells, width))
            near = jnp.zeros((cells, width), F32)
            for patch, held in zip(met, (own, first, second)):
                for r in range(rows):
                    near = jnp.where(line == patch * rows + r, held[r], near)
            total = total - coupling[l, :, f, :] * near
        driven.append(total)
    lhs = [stacked(d) for d in driven]
    chains = [(l, p) for l in range(rows) for p in range(2)]
    value, values, corr = {}, {}, {}
    for j in range(per):
        for l, p in chains:
            i = p * per + j
            r = dot_nt(lhs[l], pivots[l, i])
            d = vector(r[i : i + 1] + r[cells + i : cells + i + 1])
            if j:
                d = d + times_block(value[l, p], lower[l, i])
            value[l, p] = values[l, i] = d
    for j in reversed(range(per)):
        for l, p in chains:
            i = p * per + j
            d = values[l, i]
            if j < per - 1:
                d = d + times_block(corr[l, p], upper[l, i])
            corr[l, p] = d
            inner[l, i : i + 1, :] = d[:1]
    pad[...] = jnp.zeros(pad.shape, F32)
    ends = []
    for l in range(rows):
        for p in range(2):
            pad[l, p, :, :width] = value[l, p]
            pad[l, 2 + p, :, :width] = corr[l, p]
        f = [pad[l, 0], pad[l, 1]]
        g = [pad[l, 2], pad[l, 3]]
        v = merged_vectors(f, g, half[l, 2], tail[l, per, :high], tail[l, 0, high:])
        bias[l, 0] = f[0]
        bias[l, 1] = v[2]
        ends.append(v)
    keep[...] = jnp.zeros(keep.shape, F32)
    send[...] = jnp.zeros(send.shape, F32)
    for k in range(2):
        a, b = ends[0][k][:1, :width], ends[1][k][:1, :width]
        keep[k : k + 1, :width] = jnp.where(core == 0, a, b)
        send[k : k + 1, :width] = jnp.where(core == 0, b, a)


def side(level):
    return (lax.axis_index("line") >> level) & 1


def ordered(s, mine, theirs):
    return jnp.where(s == 0, mine, theirs), jnp.where(s == 0, theirs, mine)


def merged_maps(f, g, b, lean):
    high = f[0].shape[0]
    lhs = f[0][:, :high]
    inward = times_map(lhs, g[1])
    if lean:
        return [g[0] + times_map(inward[:, :high], b[0])], inward
    both = times_map(jnp.concatenate([inward, b[1]], axis=0)[:, :high], b[0])
    return [times_map(lhs, f[1]), g[0] + both[:high], both[high:]], inward


def merged_vectors(f, g, f_right, g_right, b_left):
    high = f_right.shape[0]
    between = times_map(f[0][:, :high], g_right) + g[1]
    return times_map(f[0][:, :high], f_right) + f[1], g[0] + times_map(between[:, :high], b_left), between


def first_maps_kernel(mine, theirs, down, full, pack):
    s = side(0)
    f, g, b = (ordered(s, mine[k], theirs[k]) for k in range(3))
    joint, inward = merged_maps(f, g, b, False)
    for k, m in enumerate([f[0], inward, b[1], f[1], g[1], b[0]]):
        down[k] = m
    size = pack.shape[0] // len(joint)
    for k, m in enumerate(joint):
        full[k] = m
        pack[k * size : (k + 1) * size] = packed(m)


def first_vectors_kernel(down, mine, theirs, out, bias):
    s = side(0)
    f = [vector(v) for v in ordered(s, mine[0:1], theirs[0:1])]
    g = [vector(v) for v in ordered(s, mine[1:2], theirs[1:2])]
    joint = merged_vectors(f, g, down[3], down[4], down[5])
    out[...] = jnp.zeros(out.shape, F32)
    out[0:1] = joint[0][:1]
    out[1:2] = joint[1][:1]
    bias[0] = f[0]
    bias[1] = joint[2]


def level_kernel(level, split, lean, mine, theirs, vectors, others, down, full, bias, out):
    high = mine.shape[1]
    size = high + 16
    maps = [unpacked(theirs[k * size : (k + 1) * size]) for k in range(3)]
    s = side(level)
    f, g, b = (ordered(s, mine[k], maps[k]) for k in range(3))
    joint, inward = merged_maps(f, g, b, lean)
    for k, m in enumerate([f[0], inward, b[1]]):
        down[k] = m
    if split:
        other = [others[0:1], others[1:2]]
    else:
        other = tail_vectors(theirs, 3 * size)
    vf = [vector(v) for v in ordered(s, vectors[0:1], other[0])]
    vg = [vector(v) for v in ordered(s, vectors[1:2], other[1])]
    v = merged_vectors(vf, vg, f[1], g[1], b[0])
    bias[0] = vf[0]
    bias[1] = v[2]
    for k, m in enumerate(joint):
        out[k * size : (k + 1) * size] = packed(m)
        if not lean:
            full[k] = m
    base = len(joint) * size
    full_vectors = jnp.concatenate([v[0][:1], v[1][:1]], axis=0)
    out[base : base + 2] = full_vectors[:, :128]
    out[base + 2 : base + 4] = full_vectors[:, 128:]
    out[base + 4 : base + 8] = jnp.zeros((4, 128), F32)
    full[full.shape[0] - 1, 0:2] = full_vectors


def tail_vectors(theirs, base):
    return [
        jnp.concatenate([theirs[base + k : base + k + 1], theirs[base + 2 + k : base + 3 + k]], axis=1)
        for k in range(2)
    ]


def top_kernel(levels, *refs):
    sides = [side(k) for k in range(levels + 1)]
    mine, theirs = refs[:2]
    downs, biases = refs[2 : levels + 2], refs[levels + 2 : 2 * levels + 2]
    keep, send = refs[-2:]
    s = sides[levels]
    size = theirs.shape[0] - 8
    high = size - 16
    g = unpacked(theirs[:size])
    other = [vector(v) for v in tail_vectors(theirs, size)]
    ours = vector(mine[mine.shape[0] - 1, 0:1])
    back = times_map(ours[:, :high], g) + other[1]
    value = jnp.where(s == 0, 0.0, other[0])
    corr = jnp.where(s == 0, back, 0.0)
    for k in reversed(range(levels)):
        d = downs[k]
        lhs = value[:, :high]
        middle = times_map(lhs, d[0]) + biases[k][0]
        back = times_map(lhs, d[1]) + times_map(corr[:, :high], d[2]) + biases[k][1]
        if k:
            value = jnp.where(sides[k] == 0, value, middle)
            corr = jnp.where(sides[k] == 0, back, corr)
    left = sides[0] == 0
    keep[0] = jnp.where(left, value, middle)
    keep[1] = jnp.where(left, back, corr)
    send[0] = jnp.where(left, middle, value)
    send[1] = jnp.where(left, corr, back)


def final_kernel(mine, theirs, inner, tail, half, bias, out):
    rows, cells, width = inner.shape
    high = half.shape[2]
    per = cells // 2
    core = side(0)
    index = lax.broadcasted_iota(jnp.int32, (8, LANES), 0)
    gathered = jnp.zeros((8, LANES), F32)
    for l in range(rows):
        y = jnp.where(core == l, mine[0], theirs[0])
        c = jnp.where(core == l, mine[1], theirs[1])
        lhs = y[:, :high]
        middle = times_map(lhs, half[l, 0]) + bias[l, 0]
        between = (
            times_map(lhs, half[l, 1])
            + times_map(c[:, :high], tail[l, per, high:])
            + bias[l, 1]
        )
        for k, v in enumerate([y, between, middle, c]):
            gathered = jnp.where(index == 4 * l + k, v, gathered)
    columns = jnp.transpose(gathered)[:high]
    for l in range(rows):
        for p in range(2):
            k = 4 * l + 2 * p
            ycol = jnp.broadcast_to(columns[:, k : k + 1], (high, 128))
            ccol = jnp.broadcast_to(columns[:, k + 1 : k + 2], (high, 128))
            col = jnp.concatenate([ycol, ccol], axis=0)
            for i in range(p * per, p * per + per):
                for h in range(2):
                    at = slice(128 * h, min(width, 128 * h + 128))
                    t = tail[l, i, :, 128 * h : 128 * h + 128] * col
                    r = jnp.sum(t, axis=0, keepdims=True)
                    out[l, i : i + 1, at] = inner[l, i : i + 1, at] + r[:, : at.stop - at.start]


def call(body, outs, specs, scratch=(), flops=None):
    return pl.pallas_call(
        body,
        out_shape=outs,
        in_specs=specs,
        out_specs=jax.tree.map(lambda _: VMEM, outs),
        scratch_shapes=scratch,
        cost_estimate=flops and pl.CostEstimate(flops=flops, bytes_accessed=0, transcendentals=0),
        compiler_params=pltpu.CompilerParams(vmem_limit_bytes=LIMIT),
    )


def f32(*shape):
    return jax.ShapeDtypeStruct(shape, F32)


def shards(right_side, previous, coupling, neighbours, pivots, lower_factor, upper_factor):
    rows, cells, width = right_side.shape
    high = width + 1
    size = high + 16
    patches = lax.axis_size("surf")
    count = lax.axis_size("line")
    levels = count.bit_length() - 1
    pairs = [(i, i + 1 - 2 * (i % 2)) for i in range(patches)]
    odd = [(i, (i - 1 + 2 * (i % 2)) % patches) for i in range(patches)]
    swap = lambda a, k: lax.ppermute(a, "line", [(i, i ^ (1 << k)) for i in range(count)])
    second = lax.ppermute(previous, "surf", odd)
    first = lax.ppermute(previous, "surf", pairs)
    full = f32(3, high, LANES)
    row = f32(8, LANES)
    unit = call(unit_kernel, [jax.ShapeDtypeStruct((high, width), BF16)], [], flops=2000000000)()[0]
    unit, lower_factor = lax.optimization_barrier((unit, lower_factor))
    ahead = call(ahead_kernel, [f32(rows, cells, high, LANES)], [VMEM] * 2, flops=12000000000)(
        unit, lower_factor
    )[0]
    ahead, upper_factor, pivots = lax.optimization_barrier((ahead, upper_factor, pivots))
    tail, half, keep, send = call(
        maps_kernel,
        [f32(rows, cells, 2 * high, LANES), f32(rows, 3, high, LANES), full, full],
        [VMEM] * 3,
        flops=12000000000,
    )(unit, ahead, upper_factor)
    send, first = lax.optimization_barrier((send, first))
    theirs = swap(send, 0)
    down, mine, pack = call(
        first_maps_kernel,
        [f32(6, high, LANES), full, f32(3 * size, 128)],
        [VMEM] * 2,
    )(keep, theirs)
    theirs = swap(pack, 1)
    inner, ends, vkeep, vsend = call(
        functools.partial(segment_kernel, patches),
        [f32(rows, cells, width), f32(rows, 2, 8, LANES), row, row],
        [VMEM] * 12,
        [pltpu.VMEM((rows, 4, 8, LANES), F32)],
        50000000000,
    )(
        neighbours, right_side, previous, first, second, coupling, pivots,
        lower_factor, upper_factor, tail, half, pack,
    )
    vtheirs = swap(vsend, 0)
    vectors, bias = call(
        first_vectors_kernel, [row, f32(2, 8, LANES)], [VMEM] * 3
    )(down, vkeep, vtheirs)
    others = swap(vectors, 1)
    downs = [down]
    biases = [bias]
    for k in range(1, levels - 1):
        lean = k == levels - 2
        down, mine, bias, pack = call(
            functools.partial(level_kernel, k, k == 1, lean),
            [
                full, f32(1 if lean else 4, high, LANES), f32(2, 8, LANES),
                f32((1 if lean else 3) * size + 8, 128),
            ],
            [VMEM] * 4,
        )(mine, theirs, vectors, others)
        downs.append(down)
        biases.append(bias)
        vectors = others = mine[-1, :8]
        theirs = swap(pack, k + 1)
    keep, send = call(
        functools.partial(top_kernel, levels - 1),
        [f32(2, 8, LANES)] * 2,
        [VMEM] * (2 + 2 * len(downs)),
    )(mine, theirs, *downs, *biases)
    return call(final_kernel, [f32(rows, cells, width)], [VMEM] * 6)(
        keep, swap(send, 0), inner, tail, half, ends
    )[0]


def solution(mesh):
    return jax.shard_map(
        shards,
        mesh=mesh,
        in_specs=(
            P("surf", "line", None),
            P("surf", "line", None),
            P("surf", "line", None, None),
            P("surf", None),
            P("surf", "line", None, None),
            P("surf", "line", None, None),
            P("surf", "line", None, None),
        ),
        out_specs=P("surf", "line", None),
        check_vma=False,
    )
```

```python
import functools

import jax
import jax.numpy as jnp
from jax import lax
from jax.experimental import pallas as pl
from jax.experimental.pallas import tpu as pltpu
from jax.sharding import PartitionSpec as P

F32 = jnp.float32
BF16 = jnp.bfloat16
VMEM = pl.BlockSpec(memory_space=pltpu.VMEM)
LANES = 256
LIMIT = 12 * 1024 * 1024


def dot_nt(a, b):
    return lax.dot_general(a, b, (((1,), (1,)), ((), ())), preferred_element_type=F32)


def dot_nn(a, b):
    return lax.dot_general(a, b, (((1,), (0,)), ((), ())), preferred_element_type=F32)


def stacked(x):
    rest = x - x.astype(BF16).astype(F32)
    return jnp.concatenate([x, rest], axis=0).astype(BF16)


def times_block(x, block):
    n = x.shape[0]
    r = dot_nt(stacked(x), block)
    return r[:n] + r[n:]


def times_map(x, m):
    n = x.shape[0]
    hi = m.astype(BF16)
    lo = (m - hi.astype(F32)).astype(BF16)
    a = stacked(x)
    r = dot_nn(a, hi)
    return r[:n] + r[n:] + dot_nn(a[:n], lo)


def vector(row):
    return jnp.broadcast_to(row, (8, row.shape[1]))


def packed(maps):
    parts = [m[:, :128] for m in maps]
    parts += [jnp.transpose(m[:128, 128:])[:8] for m in maps]
    corner = maps[0][128:, 128:]
    for k, m in enumerate(maps[1:]):
        corner = corner + pltpu.roll(m[128:, 128:], 8 * k + 8, 1)
    return jnp.concatenate(parts + [corner], axis=0)


def length(count, high):
    return count * (high + 8) + 8


def unpacked(p, count, high):
    base = count * (high + 8)
    corner = p[base : base + 8]
    lane = lax.broadcasted_iota(jnp.int32, (8, 128), 1)
    maps = []
    for k in range(count):
        top = p[count * high + 8 * k : count * high + 8 * k + 8]
        top = jnp.transpose(jnp.concatenate([top, jnp.zeros((120, 128), F32)], axis=0))
        own = pltpu.roll(corner, 128 - 8 * k, 1) if k else corner
        right = jnp.concatenate([top, jnp.where(lane < 8, own, 0.0)], axis=0)
        maps.append(jnp.concatenate([p[k * high : k * high + high], right], axis=1))
    return maps


def unit_kernel(out):
    out[...] = (
        lax.broadcasted_iota(jnp.int32, out.shape, 0) == lax.broadcasted_iota(jnp.int32, out.shape, 1)
    ).astype(BF16)


def ready_kernel(unit, lower, upper, out):
    out[...] = unit[...]


def ahead_kernel(unit, lower, ahead):
    rows, cells, width, _ = lower.shape
    per = cells // 2
    eye = unit[...]
    now = {}
    for j in range(per):
        for l in range(rows):
            for p in range(2):
                block = lower[l, p * per + j]
                if j > 1:
                    now[l, p] = times_block(now[l, p], block)
                else:
                    now[l, p] = dot_nt(now[l, p].astype(BF16) if j else eye, block)
                ahead[l, p * per + j, :, :width] = now[l, p]


def maps_kernel(unit, ahead, upper, tail, half, keep, send):
    rows, cells, width, _ = upper.shape
    high = keep.shape[1]
    per = cells // 2
    core = side(0)
    eye = unit[...]
    blank = jnp.zeros((high, LANES - 128), F32)
    for k in range(3):
        keep[k, :, 128:] = blank
        send[k, :, 128:] = blank
        for l in range(rows):
            half[l, k, :, 128:] = blank
    back = {}
    for j in reversed(range(per)):
        for l in range(rows):
            for p in range(2):
                i = p * per + j
                if j == per - 1:
                    now = jnp.concatenate(
                        [ahead[l, i, :, :width], dot_nt(eye, upper[l, i])], axis=0
                    )
                else:
                    both = times_block(back[l, p], upper[l, i])
                    now = jnp.concatenate(
                        [ahead[l, i, :, :width] + both[:high], both[high:]], axis=0
                    )
                back[l, p] = now
                tail[l, i, :, :width] = now
    joint = []
    for l in range(rows):
        f = [ahead[l, p * per + per - 1, :, :width] for p in range(2)]
        g = back[l, 0][:high], back[l, 1][:high]
        b = back[l, 0][high:], back[l, 1][high:]
        inward = times_map(f[0], g[1][:width])
        both = times_map(jnp.concatenate([inward, b[1]], axis=0), b[0][:width])
        for k, m in enumerate([f[0], inward, f[1]]):
            half[l, k, :, :width] = m
        joint.append([times_map(f[0], f[1][:width]), g[0] + both[:high], both[high:]])
    for k in range(3):
        keep[k, :, :width] = jnp.where(core == 0, joint[0][k], joint[1][k])
        send[k, :, :width] = jnp.where(core == 0, joint[1][k], joint[0][k])


def segment_kernel(
    patches, neighbours, right, own, first, second, coupling, pivots, lower, upper,
    tail, half, after, inner, bias, keep, send, pad,
):
    rows, cells, width = right.shape
    high = half.shape[2]
    per = cells // 2
    core = side(0)
    here = lax.axis_index("surf")
    odd = lax.rem(here, 2)
    after = lax.rem(here + 1, patches)
    before = lax.rem(here + patches - 1, patches)
    met = [here, jnp.where(odd == 0, after, before), jnp.where(odd == 0, before, after)]
    driven = []
    for l in range(rows):
        total = right[l]
        for f in range(coupling.shape[2]):
            line = jnp.broadcast_to(neighbours[l : l + 1, f : f + 1], (cells, width))
            near = jnp.zeros((cells, width), F32)
            for patch, held in zip(met, (own, first, second)):
                for r in range(rows):
                    near = jnp.where(line == patch * rows + r, held[r], near)
            total = total - coupling[l, :, f, :] * near
        driven.append(total)
    lhs = [stacked(d) for d in driven]
    chains = [(l, p) for l in range(rows) for p in range(2)]
    value, values, corr = {}, {}, {}
    for j in range(per):
        for l, p in chains:
            i = p * per + j
            r = dot_nt(lhs[l], pivots[l, i])
            d = vector(r[i : i + 1] + r[cells + i : cells + i + 1])
            if j:
                d = d + times_block(value[l, p], lower[l, i])
            value[l, p] = values[l, i] = d
    for j in reversed(range(per)):
        for l, p in chains:
            i = p * per + j
            d = values[l, i]
            if j < per - 1:
                d = d + times_block(corr[l, p], upper[l, i])
            corr[l, p] = d
            inner[l, i : i + 1, :] = d[:1]
    pad[...] = jnp.zeros(pad.shape, F32)
    ends = []
    for l in range(rows):
        for p in range(2):
            pad[l, p, :, :width] = value[l, p]
            pad[l, 2 + p, :, :width] = corr[l, p]
        f = [pad[l, 0], pad[l, 1]]
        g = [pad[l, 2], pad[l, 3]]
        v = merged_vectors(f, g, half[l, 2], tail[l, per, :high], tail[l, 0, high:])
        bias[l, 0] = f[0]
        bias[l, 1] = v[2]
        ends.append(v)
    keep[...] = jnp.zeros(keep.shape, F32)
    send[...] = jnp.zeros(send.shape, F32)
    for k in range(2):
        a, b = ends[0][k][:1, :width], ends[1][k][:1, :width]
        keep[k : k + 1, :width] = jnp.where(core == 0, a, b)
        send[k : k + 1, :width] = jnp.where(core == 0, b, a)


def side(level):
    return (lax.axis_index("line") >> level) & 1


def ordered(s, mine, theirs):
    return jnp.where(s == 0, mine, theirs), jnp.where(s == 0, theirs, mine)


def merged_maps(f, g, b, lean):
    high = f[0].shape[0]
    lhs = f[0][:, :high]
    inward = times_map(lhs, g[1])
    if lean:
        return [g[0] + times_map(inward[:, :high], b[0])], inward
    both = times_map(jnp.concatenate([inward, b[1]], axis=0)[:, :high], b[0])
    return [times_map(lhs, f[1]), g[0] + both[:high], both[high:]], inward


def merged_vectors(f, g, f_right, g_right, b_left):
    high = f_right.shape[0]
    between = times_map(f[0][:, :high], g_right) + g[1]
    return times_map(f[0][:, :high], f_right) + f[1], g[0] + times_map(between[:, :high], b_left), between


def first_maps_kernel(mine, theirs, down, full, pack):
    s = side(0)
    f, g, b = (ordered(s, mine[k], theirs[k]) for k in range(3))
    joint, inward = merged_maps(f, g, b, False)
    down[...] = inward
    for k, m in enumerate(joint):
        full[k] = m
    pack[...] = packed(joint)


def first_vectors_kernel(maps, others, mine, theirs, out, bias):
    s = side(0)
    f = [vector(v) for v in ordered(s, mine[0:1], theirs[0:1])]
    g = [vector(v) for v in ordered(s, mine[1:2], theirs[1:2])]
    right = [jnp.where(s == 0, others[k], maps[k]) for k in range(2)]
    joint = merged_vectors(f, g, right[0], right[1], jnp.where(s == 0, maps[2], others[2]))
    out[...] = jnp.zeros(out.shape, F32)
    out[0:1] = joint[0][:1]
    out[1:2] = joint[1][:1]
    bias[0] = f[0]
    bias[1] = joint[2]


def level_maps_kernel(level, lean, mine, theirs, down, full, pack):
    maps = unpacked(theirs, 3, mine.shape[1])
    s = side(level)
    f, g, b = (ordered(s, mine[k], maps[k]) for k in range(3))
    joint, inward = merged_maps(f, g, b, lean)
    for k, m in enumerate([f[0], inward, b[1], f[1], g[1], b[0]]):
        down[k] = m
    pack[...] = packed(joint)
    for k, m in enumerate(joint if not lean else []):
        full[k] = m


def level_vectors_kernel(level, split, down, pack, vectors, theirs, out, bias, ends):
    s = side(level)
    base = pack.shape[0]
    other = [theirs[0:1], theirs[1:2]] if split else tail_vectors(theirs, theirs.shape[0] - 8)
    vf = [vector(v) for v in ordered(s, vectors[0:1], other[0])]
    vg = [vector(v) for v in ordered(s, vectors[1:2], other[1])]
    v = merged_vectors(vf, vg, down[3], down[4], down[5])
    bias[0] = vf[0]
    bias[1] = v[2]
    both = jnp.concatenate([v[0][:1], v[1][:1]], axis=0)
    out[:base] = pack[...]
    out[base : base + 2] = both[:, :128]
    out[base + 2 : base + 4] = both[:, 128:]
    out[base + 4 : base + 8] = jnp.zeros((4, 128), F32)
    ends[0:2] = both


def tail_vectors(theirs, base):
    return [
        jnp.concatenate([theirs[base + k : base + k + 1], theirs[base + 2 + k : base + 3 + k]], axis=1)
        for k in range(2)
    ]


def top_kernel(levels, *refs):
    sides = [side(k) for k in range(levels + 1)]
    vectors, theirs, maps, others = refs[:4]
    downs, biases = refs[4 : levels + 4], refs[levels + 4 : 2 * levels + 4]
    keep, send = refs[-2:]
    s = sides[levels]
    high = maps.shape[1]
    size = length(1, high)
    g = unpacked(theirs, 1, high)[0]
    other = [vector(v) for v in tail_vectors(theirs, size)]
    ours = vector(vectors[0:1])
    back = times_map(ours[:, :high], g) + other[1]
    value = jnp.where(s == 0, 0.0, other[0])
    corr = jnp.where(s == 0, back, 0.0)
    for k in reversed(range(levels)):
        if k:
            d = downs[k]
        else:
            d = [
                jnp.where(sides[0] == 0, maps[0], others[0]),
                downs[0][...],
                jnp.where(sides[0] == 0, others[2], maps[2]),
            ]
        lhs = value[:, :high]
        middle = times_map(lhs, d[0]) + biases[k][0]
        back = times_map(lhs, d[1]) + times_map(corr[:, :high], d[2]) + biases[k][1]
        if k:
            value = jnp.where(sides[k] == 0, value, middle)
            corr = jnp.where(sides[k] == 0, back, corr)
    left = sides[0] == 0
    keep[0] = jnp.where(left, value, middle)
    keep[1] = jnp.where(left, back, corr)
    send[0] = jnp.where(left, middle, value)
    send[1] = jnp.where(left, corr, back)


def solved(line, ends, inner, tail, half, bias):
    _, cells, width = inner.shape
    high = half.shape[2]
    per = cells // 2
    y, c = ends[0], ends[1]
    lhs = y[:, :high]
    middle = times_map(lhs, half[line, 0]) + bias[line, 0]
    between = (
        times_map(lhs, half[line, 1])
        + times_map(c[:, :high], tail[line, per, high:])
        + bias[line, 1]
    )
    index = lax.broadcasted_iota(jnp.int32, (8, LANES), 0)
    gathered = jnp.zeros((8, LANES), F32)
    for k, v in enumerate([y, between, middle, c]):
        gathered = jnp.where(index == k, v, gathered)
    columns = jnp.transpose(gathered)[:high]
    parts = []
    for h in range(2):
        at = slice(128 * h, min(width, 128 * h + 128))
        sums = []
        for i in range(cells):
            k = 2 * (i // per)
            t = (
                tail[line, i, :high, 128 * h : 128 * h + 128] * columns[:, k : k + 1]
                + tail[line, i, high:, 128 * h : 128 * h + 128] * columns[:, k + 1 : k + 2]
            )
            sums.append(jnp.sum(t, axis=0, keepdims=True)[:, : at.stop - at.start])
        parts.append((at, jnp.concatenate(sums, axis=0) + inner[line, :, at]))
    return parts


def own_kernel(ends, inner, tail, half, bias, out):
    for at, value in solved(side(0), ends, inner, tail, half, bias):
        out[:, at] = value


def final_kernel(ends, own, inner, tail, half, bias, out):
    core = side(0)
    other = 1 - core
    out[core] = own[...]
    for at, value in solved(other, ends, inner, tail, half, bias):
        out[other, :, at] = value


def call(body, outs, specs, scratch=(), flops=None):
    return pl.pallas_call(
        body,
        out_shape=outs,
        in_specs=specs,
        out_specs=jax.tree.map(lambda _: VMEM, outs),
        scratch_shapes=scratch,
        cost_estimate=flops and pl.CostEstimate(flops=flops, bytes_accessed=0, transcendentals=0),
        compiler_params=pltpu.CompilerParams(vmem_limit_bytes=LIMIT),
    )


def f32(*shape):
    return jax.ShapeDtypeStruct(shape, F32)


def shards(right_side, previous, coupling, neighbours, pivots, lower_factor, upper_factor):
    rows, cells, width = right_side.shape
    high = width + 1
    patches = lax.axis_size("surf")
    count = lax.axis_size("line")
    levels = count.bit_length() - 1
    pairs = [(i, i + 1 - 2 * (i % 2)) for i in range(patches)]
    odd = [(i, (i - 1 + 2 * (i % 2)) % patches) for i in range(patches)]
    swap = lambda a, k: lax.ppermute(a, "line", [(i, i ^ (1 << k)) for i in range(count)])
    second = lax.ppermute(previous, "surf", odd)
    first = lax.ppermute(previous, "surf", pairs)
    full = f32(3, high, LANES)
    row = f32(8, LANES)
    unit = call(unit_kernel, [jax.ShapeDtypeStruct((high, width), BF16)], [], flops=2000000000)()[0]
    unit = call(ready_kernel, [jax.ShapeDtypeStruct((high, width), BF16)], [VMEM] * 3)(
        unit, jnp.transpose(lower_factor, (0, 2, 1, 3)), jnp.transpose(upper_factor, (0, 2, 1, 3))
    )[0]
    unit, lower_factor, upper_factor = lax.optimization_barrier(
        (unit, lower_factor, upper_factor)
    )
    ahead = call(ahead_kernel, [f32(rows, cells, high, LANES)], [VMEM] * 2, flops=12000000000)(
        unit, lower_factor
    )[0]
    tail, half, keep, send = call(
        maps_kernel,
        [f32(rows, cells, 2 * high, LANES), f32(rows, 3, high, LANES), full, full],
        [VMEM] * 3,
        flops=12000000000,
    )(unit, ahead, upper_factor)
    send, first = lax.optimization_barrier((send, first))
    theirs = swap(send, 0)
    first_maps = keep, theirs
    down, mine, pack = call(
        first_maps_kernel,
        [f32(high, LANES), full, f32(length(3, high), 128)],
        [VMEM] * 2,
    )(keep, theirs)
    theirs = swap(pack, 1)
    pack, pivots = lax.optimization_barrier((pack, pivots))
    inner, ends, vkeep, vsend = call(
        functools.partial(segment_kernel, patches),
        [f32(rows, cells, width), f32(rows, 2, 8, LANES), row, row],
        [VMEM] * 12,
        [pltpu.VMEM((rows, 4, 8, LANES), F32)],
        50000000000,
    )(
        neighbours, right_side, previous, first, second, coupling, pivots,
        lower_factor, upper_factor, tail, half, pack,
    )
    vtheirs = swap(vsend, 0)
    vectors, bias = call(
        first_vectors_kernel, [row, f32(2, 8, LANES)], [VMEM] * 4
    )(*first_maps, vkeep, vtheirs)
    others = swap(vectors, 1)
    downs = [down]
    biases = [bias]
    for k in range(1, levels - 1):
        lean = k == levels - 2
        count_maps = 1 if lean else 3
        down, mine, pack = call(
            functools.partial(level_maps_kernel, k, lean),
            [
                f32(6, high, LANES), f32(1 if lean else 3, high, LANES),
                f32(length(count_maps, high), 128),
            ],
            [VMEM] * 2,
            flops=20000000000,
        )(mine, theirs)
        pack, bias, vectors = call(
            functools.partial(level_vectors_kernel, k, k == 1),
            [f32(length(count_maps, high) + 8, 128), f32(2, 8, LANES), row],
            [VMEM] * 4,
        )(down, pack, vectors, others if k == 1 else theirs)
        downs.append(down)
        biases.append(bias)
        theirs = swap(pack, k + 1)
    keep, send = call(
        functools.partial(top_kernel, levels - 1),
        [f32(2, 8, LANES)] * 2,
        [VMEM] * (4 + 2 * len(downs)),
    )(vectors, theirs, *first_maps, *downs, *biases)
    theirs = swap(send, 0)
    own = call(own_kernel, [f32(cells, width)], [VMEM] * 5, flops=2000000000)(
        keep, inner, tail, half, ends
    )[0]
    return call(final_kernel, [f32(rows, cells, width)], [VMEM] * 6)(
        theirs, own, inner, tail, half, ends
    )[0]


def solution(mesh):
    return jax.shard_map(
        shards,
        mesh=mesh,
        in_specs=(
            P("surf", "line", None),
            P("surf", "line", None),
            P("surf", "line", None, None),
            P("surf", None),
            P("surf", "line", None, None),
            P("surf", "line", None, None),
            P("surf", "line", None, None),
        ),
        out_specs=P("surf", "line", None),
        check_vma=False,
    )
```

```python
import functools

import jax
import jax.numpy as jnp
from jax import lax
from jax.experimental import pallas as pl
from jax.experimental.pallas import tpu as pltpu
from jax.sharding import PartitionSpec as P

F32 = jnp.float32
BF16 = jnp.bfloat16
VMEM = pl.BlockSpec(memory_space=pltpu.VMEM)
LANES = 256
LIMIT = 12 * 1024 * 1024


def dot_nt(a, b):
    return lax.dot_general(a, b, (((1,), (1,)), ((), ())), preferred_element_type=F32)


def dot_nn(a, b):
    return lax.dot_general(a, b, (((1,), (0,)), ((), ())), preferred_element_type=F32)


def stacked(x):
    rest = x - x.astype(BF16).astype(F32)
    return jnp.concatenate([x, rest], axis=0).astype(BF16)


def times_block(x, block):
    n = x.shape[0]
    r = dot_nt(stacked(x), block)
    return r[:n] + r[n:]


def times_map(x, m):
    n = x.shape[0]
    hi = m.astype(BF16)
    lo = (m - hi.astype(F32)).astype(BF16)
    a = stacked(x)
    r = dot_nn(a, hi)
    return r[:n] + r[n:] + dot_nn(a[:n], lo)


def vector(row):
    return jnp.broadcast_to(row, (8, row.shape[1]))


def packed(maps):
    parts = [m[:, :128] for m in maps]
    parts += [jnp.transpose(m[:128, 128:])[:8] for m in maps]
    corner = maps[0][128:, 128:]
    for k, m in enumerate(maps[1:]):
        corner = corner + pltpu.roll(m[128:, 128:], 8 * k + 8, 1)
    return jnp.concatenate(parts + [corner], axis=0)


def length(count, high):
    return count * (high + 8) + 8


def unpacked(p, count, high):
    base = count * (high + 8)
    corner = p[base : base + 8]
    lane = lax.broadcasted_iota(jnp.int32, (8, 128), 1)
    maps = []
    for k in range(count):
        top = p[count * high + 8 * k : count * high + 8 * k + 8]
        top = jnp.transpose(jnp.concatenate([top, jnp.zeros((120, 128), F32)], axis=0))
        own = pltpu.roll(corner, 128 - 8 * k, 1) if k else corner
        right = jnp.concatenate([top, jnp.where(lane < 8, own, 0.0)], axis=0)
        maps.append(jnp.concatenate([p[k * high : k * high + high], right], axis=1))
    return maps


def unit_kernel(out):
    out[...] = (
        lax.broadcasted_iota(jnp.int32, out.shape, 0) == lax.broadcasted_iota(jnp.int32, out.shape, 1)
    ).astype(BF16)


def ready_kernel(unit, lower, upper, out):
    out[...] = unit[...]


def ahead_kernel(unit, lower, ahead):
    rows, cells, width, _ = lower.shape
    per = cells // 2
    eye = unit[...]
    now = {}
    for j in range(per):
        for l in range(rows):
            for p in range(2):
                block = lower[l, p * per + j]
                if j > 1:
                    now[l, p] = times_block(now[l, p], block)
                else:
                    now[l, p] = dot_nt(now[l, p].astype(BF16) if j else eye, block)
                ahead[l, p * per + j, :, :width] = now[l, p]


def maps_kernel(unit, ahead, upper, tail, half, keep, send):
    rows, cells, width, _ = upper.shape
    high = keep.shape[1]
    per = cells // 2
    core = side(0)
    eye = unit[...]
    blank = jnp.zeros((high, LANES - 128), F32)
    for k in range(3):
        keep[k, :, 128:] = blank
        send[k, :, 128:] = blank
        for l in range(rows):
            half[l, k, :, 128:] = blank
    ends = [[ahead[l, p * per + per - 1, :, :width] for p in range(2)] for l in range(rows)]
    back = {}

    def step(l, p, j):
        i = p * per + j
        if j == per - 1:
            g, b = ends[l][p], dot_nt(eye, upper[l, i])
        elif j == per - 2:
            g, b = back[l, p]
            rest = g - g.astype(BF16).astype(F32)
            r = dot_nt(jnp.concatenate([g, rest, b], axis=0).astype(BF16), upper[l, i])
            g = ahead[l, i, :, :width] + (r[:high] + r[high : 2 * high])
            b = r[2 * high :]
        else:
            both = times_block(jnp.concatenate(back[l, p], axis=0), upper[l, i])
            g = ahead[l, i, :, :width] + both[:high]
            b = both[high:]
        back[l, p] = g, b
        tail[l, i, :high, :width] = g
        tail[l, i, high:, :width] = b

    for j in reversed(range(per)):
        for p in (1, 0):
            for l in range(rows):
                step(l, p, j)
        if j == per - 1:
            front = [times_map(f[0], f[1][:width]) for f in ends]
    joint = []
    for l in range(rows):
        g = back[l, 0][0], back[l, 1][0]
        b = back[l, 0][1], back[l, 1][1]
        inward = times_map(ends[l][0], g[1][:width])
        both = times_map(jnp.concatenate([inward, b[1]], axis=0), b[0][:width])
        for k, m in enumerate([ends[l][0], inward, ends[l][1]]):
            half[l, k, :, :width] = m
        joint.append([front[l], g[0] + both[:high], both[high:]])
    for k in range(3):
        keep[k, :, :width] = jnp.where(core == 0, joint[0][k], joint[1][k])
        send[k, :, :width] = jnp.where(core == 0, joint[1][k], joint[0][k])


def segment_kernel(
    patches, neighbours, right, own, first, second, coupling, pivots, lower, upper,
    tail, half, after, inner, bias, keep, send, pad,
):
    rows, cells, width = right.shape
    high = half.shape[2]
    per = cells // 2
    core = side(0)
    here = lax.axis_index("surf")
    odd = lax.rem(here, 2)
    after = lax.rem(here + 1, patches)
    before = lax.rem(here + patches - 1, patches)
    met = [here, jnp.where(odd == 0, after, before), jnp.where(odd == 0, before, after)]
    driven = []
    for l in range(rows):
        total = right[l]
        for f in range(coupling.shape[2]):
            line = jnp.broadcast_to(neighbours[l : l + 1, f : f + 1], (cells, width))
            near = jnp.zeros((cells, width), F32)
            for patch, held in zip(met, (own, first, second)):
                for r in range(rows):
                    near = jnp.where(line == patch * rows + r, held[r], near)
            total = total - coupling[l, :, f, :] * near
        driven.append(total)
    lhs = [stacked(d) for d in driven]
    chains = [(l, p) for l in range(rows) for p in range(2)]
    value, values, corr = {}, {}, {}
    for j in range(per):
        for l, p in chains:
            i = p * per + j
            r = dot_nt(lhs[l], pivots[l, i])
            d = vector(r[i : i + 1] + r[cells + i : cells + i + 1])
            if j:
                d = d + times_block(value[l, p], lower[l, i])
            value[l, p] = values[l, i] = d
    for j in reversed(range(per)):
        for l, p in chains:
            i = p * per + j
            d = values[l, i]
            if j < per - 1:
                d = d + times_block(corr[l, p], upper[l, i])
            corr[l, p] = d
            inner[l, i : i + 1, :] = d[:1]
    pad[...] = jnp.zeros(pad.shape, F32)
    ends = []
    for l in range(rows):
        for p in range(2):
            pad[l, p, :, :width] = value[l, p]
            pad[l, 2 + p, :, :width] = corr[l, p]
        f = [pad[l, 0], pad[l, 1]]
        g = [pad[l, 2], pad[l, 3]]
        v = merged_vectors(f, g, half[l, 2], tail[l, per, :high], tail[l, 0, high:])
        bias[l, 0] = f[0]
        bias[l, 1] = v[2]
        ends.append(v)
    keep[...] = jnp.zeros(keep.shape, F32)
    send[...] = jnp.zeros(send.shape, F32)
    for k in range(2):
        a, b = ends[0][k][:1, :width], ends[1][k][:1, :width]
        keep[k : k + 1, :width] = jnp.where(core == 0, a, b)
        send[k : k + 1, :width] = jnp.where(core == 0, b, a)


def side(level):
    return (lax.axis_index("line") >> level) & 1


def ordered(s, mine, theirs):
    return jnp.where(s == 0, mine, theirs), jnp.where(s == 0, theirs, mine)


def merged_maps(f, g, b):
    high = f[0].shape[0]
    lhs = f[0][:, :high]
    inward = times_map(lhs, g[1])
    both = times_map(jnp.concatenate([inward, b[1]], axis=0)[:, :high], b[0])
    return [times_map(lhs, f[1]), g[0] + both[:high], both[high:]], inward


def merged_vectors(f, g, f_right, g_right, b_left):
    high = f_right.shape[0]
    between = times_map(f[0][:, :high], g_right) + g[1]
    return times_map(f[0][:, :high], f_right) + f[1], g[0] + times_map(between[:, :high], b_left), between


def first_maps_kernel(mine, theirs, down, full, pack):
    s = side(0)
    f, g, b = (ordered(s, mine[k], theirs[k]) for k in range(3))
    joint, inward = merged_maps(f, g, b)
    down[...] = inward
    for k, m in enumerate(joint):
        full[k] = m
    pack[...] = packed(joint)


def first_vectors_kernel(maps, others, mine, theirs, out, bias):
    s = side(0)
    f = [vector(v) for v in ordered(s, mine[0:1], theirs[0:1])]
    g = [vector(v) for v in ordered(s, mine[1:2], theirs[1:2])]
    right = [jnp.where(s == 0, others[k], maps[k]) for k in range(2)]
    joint = merged_vectors(f, g, right[0], right[1], jnp.where(s == 0, maps[2], others[2]))
    out[...] = jnp.zeros(out.shape, F32)
    out[0:1] = joint[0][:1]
    out[1:2] = joint[1][:1]
    bias[0] = f[0]
    bias[1] = joint[2]


def level_maps_kernel(level, lean, mine, theirs, down, full, pack):
    high = mine.shape[1]
    maps = unpacked(theirs, 3, high)
    s = side(level)
    f, g, b = (ordered(s, mine[k], maps[k]) for k in range(3))
    lhs = f[0][:, :high]
    if lean:
        through = times_map(g[1][:, :high], b[0])
        joint = [g[0] + times_map(lhs, through)]
    else:
        both = times_map(jnp.concatenate([g[1], b[1]], axis=0)[:, :high], b[0])
        through = both[:high]
        joint = [times_map(lhs, f[1]), g[0] + times_map(lhs, through), both[high:]]
    pack[...] = packed(joint)
    for k, m in enumerate([f[0], b[1], f[1], g[1], b[0], through]):
        down[k] = m
    for k, m in enumerate(joint if not lean else []):
        full[k] = m


def level_vectors_kernel(level, split, down, pack, vectors, theirs, out, bias, ends):
    s = side(level)
    base = pack.shape[0]
    other = [theirs[0:1], theirs[1:2]] if split else tail_vectors(theirs, theirs.shape[0] - 8)
    vf = [vector(v) for v in ordered(s, vectors[0:1], other[0])]
    vg = [vector(v) for v in ordered(s, vectors[1:2], other[1])]
    high = down.shape[1]
    lhs = vf[0][:, :high]
    v = (
        times_map(lhs, down[2]) + vf[1],
        vg[0] + times_map(lhs, down[5]) + times_map(vg[1][:, :high], down[4]),
        times_map(lhs, down[3]) + vg[1],
    )
    bias[0] = vf[0]
    bias[1] = v[2]
    both = jnp.concatenate([v[0][:1], v[1][:1]], axis=0)
    out[:base] = pack[...]
    out[base : base + 2] = both[:, :128]
    out[base + 2 : base + 4] = both[:, 128:]
    out[base + 4 : base + 8] = jnp.zeros((4, 128), F32)
    ends[0:2] = both


def tail_vectors(theirs, base):
    return [
        jnp.concatenate([theirs[base + k : base + k + 1], theirs[base + 2 + k : base + 3 + k]], axis=1)
        for k in range(2)
    ]


def paths_kernel(levels, *refs):
    maps, others, first_inward = refs[:3]
    downs, biases = refs[3 : levels + 2], refs[levels + 2 : 2 * levels + 2]
    hi, lo, add = refs[-3:]
    high = maps.shape[1]
    top = side(levels) == 1
    s = side(0)
    eye = (
        lax.broadcasted_iota(jnp.int32, (high, LANES), 0)
        == lax.broadcasted_iota(jnp.int32, (high, LANES), 1)
    ).astype(F32)
    nothing = jnp.zeros((8, LANES), F32)
    value = jnp.concatenate([jnp.where(top, eye, 0.0), nothing], axis=0)
    corr = jnp.concatenate([jnp.where(top, 0.0, eye), nothing], axis=0)
    for k in reversed(range(levels)):
        if k:
            d = downs[k - 1]
            f, b = d[0], d[1]
            inward = times_map(f[:, :high], d[3])
        else:
            f = jnp.where(s == 0, maps[0], others[0])
            b = jnp.where(s == 0, others[2], maps[2])
            inward = first_inward[...]
        if k == levels - 1:
            middle, back = jnp.where(top, f, 0.0), jnp.where(top, inward, b)
            middle = jnp.concatenate([middle, nothing], axis=0)
            back = jnp.concatenate([back, nothing], axis=0)
        else:
            lhs = value[:, :high]
            middle = times_map(lhs, f)
            back = times_map(lhs, inward) + times_map(corr[:, :high], b)
        base = jnp.zeros((high, LANES), F32)
        middle = middle + jnp.concatenate([base, biases[k][0]], axis=0)
        back = back + jnp.concatenate([base, biases[k][1]], axis=0)
        if k:
            value = jnp.where(side(k) == 0, value, middle)
            corr = jnp.where(side(k) == 0, back, corr)
    paths = [
        jnp.where(s == 0, value, middle), jnp.where(s == 0, back, corr),
        jnp.where(s == 0, middle, value), jnp.where(s == 0, corr, back),
    ]
    for k, m in enumerate(paths):
        top_term = m[:high].astype(BF16)
        hi[k] = top_term
        lo[k] = (m[:high] - top_term.astype(F32)).astype(BF16)
        add[k] = m[high:]


def top_kernel(level, vectors, theirs, hi, lo, add, keep, send):
    high = hi.shape[1]
    g = unpacked(theirs, 1, high)[0]
    other = [vector(v) for v in tail_vectors(theirs, length(1, high))]
    ours = vector(vectors[0:1])
    back = times_map(ours[:, :high], g) + other[1]
    x = jnp.where(side(level) == 0, back, other[0])[:, :high]
    a = stacked(x)
    for k in range(4):
        r = dot_nn(a, hi[k])
        r = r[:8] + r[8:] + dot_nn(a[:8], lo[k]) + add[k]
        if k < 2:
            keep[k] = r
        else:
            send[k - 2] = r


def solved(line, ends, inner, tail, half, bias):
    _, cells, width = inner.shape
    high = half.shape[2]
    per = cells // 2
    y, c = ends[0], ends[1]
    lhs = y[:, :high]
    middle = times_map(lhs, half[line, 0]) + bias[line, 0]
    between = (
        times_map(lhs, half[line, 1])
        + times_map(c[:, :high], tail[line, per, high:])
        + bias[line, 1]
    )
    index = lax.broadcasted_iota(jnp.int32, (8, LANES), 0)
    gathered = jnp.zeros((8, LANES), F32)
    for k, v in enumerate([y, between, middle, c]):
        gathered = jnp.where(index == k, v, gathered)
    columns = jnp.transpose(gathered)[:high]
    parts = []
    for h in range(2):
        at = slice(128 * h, min(width, 128 * h + 128))
        sums = []
        for i in range(cells):
            k = 2 * (i // per)
            t = (
                tail[line, i, :high, 128 * h : 128 * h + 128] * columns[:, k : k + 1]
                + tail[line, i, high:, 128 * h : 128 * h + 128] * columns[:, k + 1 : k + 2]
            )
            sums.append(jnp.sum(t, axis=0, keepdims=True)[:, : at.stop - at.start])
        parts.append((at, jnp.concatenate(sums, axis=0) + inner[line, :, at]))
    return parts


def own_kernel(ends, inner, tail, half, bias, out):
    for at, value in solved(side(0), ends, inner, tail, half, bias):
        out[:, at] = value


def final_kernel(ends, own, inner, tail, half, bias, out):
    core = side(0)
    other = 1 - core
    out[core] = own[...]
    for at, value in solved(other, ends, inner, tail, half, bias):
        out[other, :, at] = value


def call(body, outs, specs, scratch=(), flops=None):
    return pl.pallas_call(
        body,
        out_shape=outs,
        in_specs=specs,
        out_specs=jax.tree.map(lambda _: VMEM, outs),
        scratch_shapes=scratch,
        cost_estimate=flops and pl.CostEstimate(flops=flops, bytes_accessed=0, transcendentals=0),
        compiler_params=pltpu.CompilerParams(vmem_limit_bytes=LIMIT),
    )


def f32(*shape):
    return jax.ShapeDtypeStruct(shape, F32)


def shards(right_side, previous, coupling, neighbours, pivots, lower_factor, upper_factor):
    rows, cells, width = right_side.shape
    high = width + 1
    patches = lax.axis_size("surf")
    count = lax.axis_size("line")
    levels = count.bit_length() - 1
    pairs = [(i, i + 1 - 2 * (i % 2)) for i in range(patches)]
    odd = [(i, (i - 1 + 2 * (i % 2)) % patches) for i in range(patches)]
    swap = lambda a, k: lax.ppermute(a, "line", [(i, i ^ (1 << k)) for i in range(count)])
    second = lax.ppermute(previous, "surf", odd)
    first = lax.ppermute(previous, "surf", pairs)
    full = f32(3, high, LANES)
    row = f32(8, LANES)
    unit = call(unit_kernel, [jax.ShapeDtypeStruct((high, width), BF16)], [], flops=2000000000)()[0]
    unit = call(ready_kernel, [jax.ShapeDtypeStruct((high, width), BF16)], [VMEM] * 3)(
        unit, jnp.transpose(lower_factor, (0, 2, 1, 3)), jnp.transpose(upper_factor, (0, 2, 1, 3))
    )[0]
    unit, lower_factor, upper_factor = lax.optimization_barrier(
        (unit, lower_factor, upper_factor)
    )
    ahead = call(ahead_kernel, [f32(rows, cells, high, LANES)], [VMEM] * 2, flops=12000000000)(
        unit, lower_factor
    )[0]
    tail, half, keep, send = call(
        maps_kernel,
        [f32(rows, cells, 2 * high, LANES), f32(rows, 3, high, LANES), full, full],
        [VMEM] * 3,
        flops=12000000000,
    )(unit, ahead, upper_factor)
    send, first = lax.optimization_barrier((send, first))
    theirs = swap(send, 0)
    first_maps = keep, theirs
    down, mine, pack = call(
        first_maps_kernel,
        [f32(high, LANES), full, f32(length(3, high), 128)],
        [VMEM] * 2,
    )(keep, theirs)
    theirs = swap(pack, 1)
    pack, pivots = lax.optimization_barrier((pack, pivots))
    inner, ends, vkeep, vsend = call(
        functools.partial(segment_kernel, patches),
        [f32(rows, cells, width), f32(rows, 2, 8, LANES), row, row],
        [VMEM] * 12,
        [pltpu.VMEM((rows, 4, 8, LANES), F32)],
        50000000000,
    )(
        neighbours, right_side, previous, first, second, coupling, pivots,
        lower_factor, upper_factor, tail, half, pack,
    )
    vtheirs = swap(vsend, 0)
    vectors, bias = call(
        first_vectors_kernel, [row, f32(2, 8, LANES)], [VMEM] * 4
    )(*first_maps, vkeep, vtheirs)
    others = swap(vectors, 1)
    downs = [down]
    biases = [bias]
    for k in range(1, levels - 1):
        lean = k == levels - 2
        count_maps = 1 if lean else 3
        down, mine, pack = call(
            functools.partial(level_maps_kernel, k, lean),
            [
                f32(6, high, LANES), f32(1 if lean else 3, high, LANES),
                f32(length(count_maps, high), 128),
            ],
            [VMEM] * 2,
            flops=20000000000,
        )(mine, theirs)
        pack, bias, vectors = call(
            functools.partial(level_vectors_kernel, k, k == 1),
            [f32(length(count_maps, high) + 8, 128), f32(2, 8, LANES), row],
            [VMEM] * 4,
        )(down, pack, vectors, others if k == 1 else theirs)
        downs.append(down)
        biases.append(bias)
        theirs = swap(pack, k + 1)
    hi, lo, add = call(
        functools.partial(paths_kernel, levels - 1),
        [jax.ShapeDtypeStruct((4, high, LANES), BF16)] * 2 + [f32(4, 8, LANES)],
        [VMEM] * (2 + len(downs) + len(biases)),
        flops=3000000000,
    )(*first_maps, *downs, *biases)
    keep, send = call(
        functools.partial(top_kernel, levels - 1), [f32(2, 8, LANES)] * 2, [VMEM] * 5
    )(vectors, theirs, hi, lo, add)
    theirs = swap(send, 0)
    own = call(own_kernel, [f32(cells, width)], [VMEM] * 5, flops=2000000000)(
        keep, inner, tail, half, ends
    )[0]
    return call(final_kernel, [f32(rows, cells, width)], [VMEM] * 6)(
        theirs, own, inner, tail, half, ends
    )[0]


def solution(mesh):
    return jax.shard_map(
        shards,
        mesh=mesh,
        in_specs=(
            P("surf", "line", None),
            P("surf", "line", None),
            P("surf", "line", None, None),
            P("surf", None),
            P("surf", "line", None, None),
            P("surf", "line", None, None),
            P("surf", "line", None, None),
        ),
        out_specs=P("surf", "line", None),
        check_vma=False,
    )
```

```python
import functools

import jax
import jax.numpy as jnp
from jax import lax
from jax.experimental import pallas as pl
from jax.experimental.pallas import tpu as pltpu
from jax.sharding import PartitionSpec as P

F32 = jnp.float32
BF16 = jnp.bfloat16
VMEM = pl.BlockSpec(memory_space=pltpu.VMEM)
LANES = 256
LIMIT = 12 * 1024 * 1024


def dot_nt(a, b):
    return lax.dot_general(a, b, (((1,), (1,)), ((), ())), preferred_element_type=F32)


def dot_nn(a, b):
    return lax.dot_general(a, b, (((1,), (0,)), ((), ())), preferred_element_type=F32)


def stacked(x):
    rest = x - x.astype(BF16).astype(F32)
    return jnp.concatenate([x, rest], axis=0).astype(BF16)


def times_block(x, block):
    n = x.shape[0]
    r = dot_nt(stacked(x), block)
    return r[:n] + r[n:]


def times_map(x, m):
    n = x.shape[0]
    hi = m.astype(BF16)
    lo = (m - hi.astype(F32)).astype(BF16)
    a = stacked(x)
    r = dot_nn(a, hi)
    return r[:n] + r[n:] + dot_nn(a[:n], lo)


def vector(row):
    return jnp.broadcast_to(row, (8, row.shape[1]))


def packed(maps):
    parts = [m[:, :128] for m in maps]
    parts += [jnp.transpose(m[:128, 128:])[:8] for m in maps]
    corner = maps[0][128:, 128:]
    for k, m in enumerate(maps[1:]):
        corner = corner + pltpu.roll(m[128:, 128:], 8 * k + 8, 1)
    return jnp.concatenate(parts + [corner], axis=0)


def length(count, high):
    return count * (high + 8) + 8


def unpacked(p, count, high):
    base = count * (high + 8)
    corner = p[base : base + 8]
    lane = lax.broadcasted_iota(jnp.int32, (8, 128), 1)
    maps = []
    for k in range(count):
        top = p[count * high + 8 * k : count * high + 8 * k + 8]
        top = jnp.transpose(jnp.concatenate([top, jnp.zeros((120, 128), F32)], axis=0))
        own = pltpu.roll(corner, 128 - 8 * k, 1) if k else corner
        right = jnp.concatenate([top, jnp.where(lane < 8, own, 0.0)], axis=0)
        maps.append(jnp.concatenate([p[k * high : k * high + high], right], axis=1))
    return maps


def unit_kernel(out):
    out[...] = (
        lax.broadcasted_iota(jnp.int32, out.shape, 0) == lax.broadcasted_iota(jnp.int32, out.shape, 1)
    ).astype(BF16)


def ready_kernel(unit, lower, upper, out):
    out[...] = unit[...]


def ahead_kernel(unit, lower, ahead):
    rows, cells, width, _ = lower.shape
    per = cells // 2
    eye = unit[...]
    now = {}
    for j in range(per):
        for l in range(rows):
            for p in range(2):
                block = lower[l, p * per + j]
                if j > 1:
                    now[l, p] = times_block(now[l, p], block)
                else:
                    now[l, p] = dot_nt(now[l, p].astype(BF16) if j else eye, block)
                ahead[l, p * per + j, :, :width] = now[l, p]


def maps_kernel(unit, ahead, upper, tail, half, keep, send):
    rows, cells, width, _ = upper.shape
    high = keep.shape[1]
    per = cells // 2
    core = side(0)
    eye = unit[...]
    blank = jnp.zeros((high, LANES - 128), F32)
    for k in range(3):
        keep[k, :, 128:] = blank
        send[k, :, 128:] = blank
        for l in range(rows):
            half[l, k, :, 128:] = blank
    ends = [[ahead[l, p * per + per - 1, :, :width] for p in range(2)] for l in range(rows)]
    back = {}

    def step(l, p, j):
        i = p * per + j
        if j == per - 1:
            g, b = ends[l][p], dot_nt(eye, upper[l, i])
        elif j == per - 2:
            g, b = back[l, p]
            rest = g - g.astype(BF16).astype(F32)
            r = dot_nt(jnp.concatenate([g, rest, b], axis=0).astype(BF16), upper[l, i])
            g = ahead[l, i, :, :width] + (r[:high] + r[high : 2 * high])
            b = r[2 * high :]
        else:
            both = times_block(jnp.concatenate(back[l, p], axis=0), upper[l, i])
            g = ahead[l, i, :, :width] + both[:high]
            b = both[high:]
        back[l, p] = g, b
        tail[l, i, :high, :width] = g
        tail[l, i, high:, :width] = b

    for j in reversed(range(per)):
        for p in (1, 0):
            for l in range(rows):
                step(l, p, j)
        if j == per - 1:
            front = [times_map(f[0], f[1][:width]) for f in ends]
    joint = []
    for l in range(rows):
        g = back[l, 0][0], back[l, 1][0]
        b = back[l, 0][1], back[l, 1][1]
        inward = times_map(ends[l][0], g[1][:width])
        both = times_map(jnp.concatenate([inward, b[1]], axis=0), b[0][:width])
        for k, m in enumerate([ends[l][0], inward, ends[l][1]]):
            half[l, k, :, :width] = m
        joint.append([front[l], g[0] + both[:high], both[high:]])
    for k in range(3):
        keep[k, :, :width] = jnp.where(core == 0, joint[0][k], joint[1][k])
        send[k, :, :width] = jnp.where(core == 0, joint[1][k], joint[0][k])


def segment_kernel(
    patches, neighbours, right, own, first, second, coupling, pivots, lower, upper,
    tail, half, after, inner, bias, keep, send, pad,
):
    rows, cells, width = right.shape
    high = half.shape[2]
    per = cells // 2
    core = side(0)
    here = lax.axis_index("surf")
    odd = lax.rem(here, 2)
    after = lax.rem(here + 1, patches)
    before = lax.rem(here + patches - 1, patches)
    met = [here, jnp.where(odd == 0, after, before), jnp.where(odd == 0, before, after)]
    driven = []
    for l in range(rows):
        total = right[l]
        for f in range(coupling.shape[2]):
            line = jnp.broadcast_to(neighbours[l : l + 1, f : f + 1], (cells, width))
            near = jnp.zeros((cells, width), F32)
            for patch, held in zip(met, (own, first, second)):
                for r in range(rows):
                    near = jnp.where(line == patch * rows + r, held[r], near)
            total = total - coupling[l, :, f, :] * near
        driven.append(total)
    lhs = [stacked(d) for d in driven]
    chains = [(l, p) for l in range(rows) for p in range(2)]
    value, values, corr = {}, {}, {}
    for j in range(per):
        for l, p in chains:
            i = p * per + j
            r = dot_nt(lhs[l], pivots[l, i])
            d = vector(r[i : i + 1] + r[cells + i : cells + i + 1])
            if j:
                d = d + times_block(value[l, p], lower[l, i])
            value[l, p] = values[l, i] = d
    for j in reversed(range(per)):
        for l, p in chains:
            i = p * per + j
            d = values[l, i]
            if j < per - 1:
                d = d + times_block(corr[l, p], upper[l, i])
            corr[l, p] = d
            inner[l, i : i + 1, :] = d[:1]
    pad[...] = jnp.zeros(pad.shape, F32)
    ends = []
    for l in range(rows):
        for p in range(2):
            pad[l, p, :, :width] = value[l, p]
            pad[l, 2 + p, :, :width] = corr[l, p]
        f = [pad[l, 0], pad[l, 1]]
        g = [pad[l, 2], pad[l, 3]]
        v = merged_vectors(f, g, half[l, 2], tail[l, per, :high], tail[l, 0, high:])
        bias[l, 0] = f[0]
        bias[l, 1] = v[2]
        ends.append(v)
    keep[...] = jnp.zeros(keep.shape, F32)
    send[...] = jnp.zeros(send.shape, F32)
    for k in range(2):
        a, b = ends[0][k][:1, :width], ends[1][k][:1, :width]
        keep[k : k + 1, :width] = jnp.where(core == 0, a, b)
        send[k : k + 1, :width] = jnp.where(core == 0, b, a)


def side(level):
    return (lax.axis_index("line") >> level) & 1


def ordered(s, mine, theirs):
    return jnp.where(s == 0, mine, theirs), jnp.where(s == 0, theirs, mine)


def merged_maps(f, g, b):
    high = f[0].shape[0]
    lhs = f[0][:, :high]
    inward = times_map(lhs, g[1])
    both = times_map(jnp.concatenate([inward, b[1]], axis=0)[:, :high], b[0])
    return [times_map(lhs, f[1]), g[0] + both[:high], both[high:]], inward


def merged_vectors(f, g, f_right, g_right, b_left):
    high = f_right.shape[0]
    between = times_map(f[0][:, :high], g_right) + g[1]
    return times_map(f[0][:, :high], f_right) + f[1], g[0] + times_map(between[:, :high], b_left), between


def first_maps_kernel(mine, theirs, down, full, pack):
    s = side(0)
    f, g, b = (ordered(s, mine[k], theirs[k]) for k in range(3))
    joint, inward = merged_maps(f, g, b)
    down[...] = inward
    for k, m in enumerate(joint):
        full[k] = m
    pack[...] = packed(joint)


def first_vectors_kernel(maps, others, mine, theirs, out, bias):
    s = side(0)
    f = [vector(v) for v in ordered(s, mine[0:1], theirs[0:1])]
    g = [vector(v) for v in ordered(s, mine[1:2], theirs[1:2])]
    right = [jnp.where(s == 0, others[k], maps[k]) for k in range(2)]
    joint = merged_vectors(f, g, right[0], right[1], jnp.where(s == 0, maps[2], others[2]))
    out[...] = jnp.zeros(out.shape, F32)
    out[0:1] = joint[0][:1]
    out[1:2] = joint[1][:1]
    bias[0] = f[0]
    bias[1] = joint[2]


def level_maps_kernel(level, lean, mine, theirs, down, pack, full=None):
    high = mine.shape[1]
    maps = unpacked(theirs, 3, high)
    s = side(level)
    f, g, b = (ordered(s, mine[k], maps[k]) for k in range(3))
    lhs = f[0][:, :high]
    if lean:
        through = times_map(g[1][:, :high], b[0])
        joint = [g[0] + times_map(lhs, through)]
    else:
        both = times_map(jnp.concatenate([g[1], b[1]], axis=0)[:, :high], b[0])
        through = both[:high]
        joint = [times_map(lhs, f[1]), g[0] + times_map(lhs, through), both[high:]]
    pack[...] = packed(joint)
    for k, m in enumerate([f[0], b[1], f[1], g[1], b[0], through]):
        down[k] = m
    for k, m in enumerate(joint if not lean else []):
        full[k] = m


def level_vectors_kernel(level, split, down, pack, vectors, theirs, out, bias, ends):
    s = side(level)
    base = pack.shape[0]
    other = [theirs[0:1], theirs[1:2]] if split else tail_vectors(theirs, theirs.shape[0] - 8)
    vf = [vector(v) for v in ordered(s, vectors[0:1], other[0])]
    vg = [vector(v) for v in ordered(s, vectors[1:2], other[1])]
    high = down.shape[1]
    lhs = vf[0][:, :high]
    v = (
        times_map(lhs, down[2]) + vf[1],
        vg[0] + times_map(lhs, down[5]) + times_map(vg[1][:, :high], down[4]),
        times_map(lhs, down[3]) + vg[1],
    )
    bias[0] = vf[0]
    bias[1] = v[2]
    both = jnp.concatenate([v[0][:1], v[1][:1]], axis=0)
    out[:base] = pack[...]
    out[base : base + 2] = both[:, :128]
    out[base + 2 : base + 4] = both[:, 128:]
    out[base + 4 : base + 8] = jnp.zeros((4, 128), F32)
    ends[0:2] = both


def tail_vectors(theirs, base):
    return [
        jnp.concatenate([theirs[base + k : base + k + 1], theirs[base + 2 + k : base + 3 + k]], axis=1)
        for k in range(2)
    ]


def paths_kernel(levels, *refs):
    maps, others, first_inward = refs[:3]
    downs, biases = refs[3 : levels + 2], refs[levels + 2 : 2 * levels + 2]
    hi, lo, add = refs[-3:]
    high = maps.shape[1]
    top = side(levels) == 1
    s = side(0)
    eye = (
        lax.broadcasted_iota(jnp.int32, (high, LANES), 0)
        == lax.broadcasted_iota(jnp.int32, (high, LANES), 1)
    ).astype(F32)
    nothing = jnp.zeros((8, LANES), F32)
    value = jnp.concatenate([jnp.where(top, eye, 0.0), nothing], axis=0)
    corr = jnp.concatenate([jnp.where(top, 0.0, eye), nothing], axis=0)
    for k in reversed(range(levels)):
        if k:
            d = downs[k - 1]
            f, b = d[0], d[1]
            inward = times_map(f[:, :high], d[3])
        else:
            f = jnp.where(s == 0, maps[0], others[0])
            b = jnp.where(s == 0, others[2], maps[2])
            inward = first_inward[...]
        if k == levels - 1:
            middle, back = jnp.where(top, f, 0.0), jnp.where(top, inward, b)
            middle = jnp.concatenate([middle, nothing], axis=0)
            back = jnp.concatenate([back, nothing], axis=0)
        else:
            lhs = value[:, :high]
            middle = times_map(lhs, f)
            back = times_map(lhs, inward) + times_map(corr[:, :high], b)
        base = jnp.zeros((high, LANES), F32)
        middle = middle + jnp.concatenate([base, biases[k][0]], axis=0)
        back = back + jnp.concatenate([base, biases[k][1]], axis=0)
        if k:
            value = jnp.where(side(k) == 0, value, middle)
            corr = jnp.where(side(k) == 0, back, corr)
    paths = [
        jnp.where(s == 0, value, middle), jnp.where(s == 0, back, corr),
        jnp.where(s == 0, middle, value), jnp.where(s == 0, corr, back),
    ]
    for k, m in enumerate(paths):
        top_term = m[:high].astype(BF16)
        hi[k] = top_term
        lo[k] = (m[:high] - top_term.astype(F32)).astype(BF16)
        add[k] = m[high:]


def top_kernel(level, vectors, theirs, hi, lo, add, keep, send):
    high = hi.shape[1]
    g = unpacked(theirs, 1, high)[0]
    other = [vector(v) for v in tail_vectors(theirs, length(1, high))]
    ours = vector(vectors[0:1])
    back = times_map(ours[:, :high], g) + other[1]
    x = jnp.where(side(level) == 0, back, other[0])[:, :high]
    a = stacked(x)
    for k in range(4):
        r = dot_nn(a, hi[k])
        r = r[:8] + r[8:] + dot_nn(a[:8], lo[k]) + add[k]
        if k < 2:
            keep[k] = r
        else:
            send[k - 2] = r


def solved(line, ends, inner, tail, half, bias):
    _, cells, width = inner.shape
    high = half.shape[2]
    per = cells // 2
    y, c = ends[0], ends[1]
    lhs = y[:, :high]
    middle = times_map(lhs, half[line, 0]) + bias[line, 0]
    between = (
        times_map(lhs, half[line, 1])
        + times_map(c[:, :high], tail[line, per, high:])
        + bias[line, 1]
    )
    index = lax.broadcasted_iota(jnp.int32, (8, LANES), 0)
    gathered = jnp.zeros((8, LANES), F32)
    for k, v in enumerate([y, between, middle, c]):
        gathered = jnp.where(index == k, v, gathered)
    columns = jnp.transpose(gathered)[:high]
    columns = [jnp.broadcast_to(columns[:, k : k + 1], (high, 128)) for k in range(4)]
    parts = []
    for h in range(2):
        at = slice(128 * h, min(width, 128 * h + 128))
        sums = []
        for i in range(cells):
            k = 2 * (i // per)
            t = (
                tail[line, i, :high, 128 * h : 128 * h + 128] * columns[k]
                + tail[line, i, high:, 128 * h : 128 * h + 128] * columns[k + 1]
            )
            sums.append(jnp.sum(t, axis=0, keepdims=True)[:, : at.stop - at.start])
        parts.append((at, jnp.concatenate(sums, axis=0) + inner[line, :, at]))
    return parts


def own_kernel(ends, inner, tail, half, bias, out):
    for at, value in solved(side(0), ends, inner, tail, half, bias):
        out[:, at] = value


def final_kernel(ends, own, inner, tail, half, bias, out):
    core = side(0)
    other = 1 - core
    out[core] = own[...]
    for at, value in solved(other, ends, inner, tail, half, bias):
        out[other, :, at] = value


def call(body, outs, specs, scratch=(), flops=None):
    return pl.pallas_call(
        body,
        out_shape=outs,
        in_specs=specs,
        out_specs=jax.tree.map(lambda _: VMEM, outs),
        scratch_shapes=scratch,
        cost_estimate=flops and pl.CostEstimate(flops=flops, bytes_accessed=0, transcendentals=0),
        compiler_params=pltpu.CompilerParams(vmem_limit_bytes=LIMIT),
    )


def f32(*shape):
    return jax.ShapeDtypeStruct(shape, F32)


def shards(right_side, previous, coupling, neighbours, pivots, lower_factor, upper_factor):
    rows, cells, width = right_side.shape
    high = width + 1
    patches = lax.axis_size("surf")
    count = lax.axis_size("line")
    levels = count.bit_length() - 1
    pairs = [(i, i + 1 - 2 * (i % 2)) for i in range(patches)]
    odd = [(i, (i - 1 + 2 * (i % 2)) % patches) for i in range(patches)]
    swap = lambda a, k: lax.ppermute(a, "line", [(i, i ^ (1 << k)) for i in range(count)])
    second = lax.ppermute(previous, "surf", odd)
    first = lax.ppermute(previous, "surf", pairs)
    full = f32(3, high, LANES)
    row = f32(8, LANES)
    unit = call(unit_kernel, [jax.ShapeDtypeStruct((high, width), BF16)], [], flops=2000000000)()[0]
    unit = call(ready_kernel, [jax.ShapeDtypeStruct((high, width), BF16)], [VMEM] * 3)(
        unit, jnp.transpose(lower_factor, (0, 2, 1, 3)), jnp.transpose(upper_factor, (0, 2, 1, 3))
    )[0]
    unit, lower_factor, upper_factor = lax.optimization_barrier(
        (unit, lower_factor, upper_factor)
    )
    ahead = call(ahead_kernel, [f32(rows, cells, high, LANES)], [VMEM] * 2, flops=12000000000)(
        unit, lower_factor
    )[0]
    tail, half, keep, send = call(
        maps_kernel,
        [f32(rows, cells, 2 * high, LANES), f32(rows, 3, high, LANES), full, full],
        [VMEM] * 3,
        flops=12000000000,
    )(unit, ahead, upper_factor)
    send, first = lax.optimization_barrier((send, first))
    theirs = swap(send, 0)
    first_maps = keep, theirs
    down, mine, pack = call(
        first_maps_kernel,
        [f32(high, LANES), full, f32(length(3, high), 128)],
        [VMEM] * 2,
    )(keep, theirs)
    theirs = swap(pack, 1)
    pack, pivots = lax.optimization_barrier((pack, pivots))
    inner, ends, vkeep, vsend = call(
        functools.partial(segment_kernel, patches),
        [f32(rows, cells, width), f32(rows, 2, 8, LANES), row, row],
        [VMEM] * 12,
        [pltpu.VMEM((rows, 4, 8, LANES), F32)],
        50000000000,
    )(
        neighbours, right_side, previous, first, second, coupling, pivots,
        lower_factor, upper_factor, tail, half, pack,
    )
    vtheirs = swap(vsend, 0)
    vectors, bias = call(
        first_vectors_kernel, [row, f32(2, 8, LANES)], [VMEM] * 4
    )(*first_maps, vkeep, vtheirs)
    others = swap(vectors, 1)
    downs = [down]
    biases = [bias]
    for k in range(1, levels - 1):
        lean = k == levels - 2
        count_maps = 1 if lean else 3
        down, pack, *joint = call(
            functools.partial(level_maps_kernel, k, lean),
            [
                f32(6, high, LANES), f32(length(count_maps, high), 128),
            ] + ([] if lean else [full]),
            [VMEM] * 2,
            flops=20000000000,
        )(mine, theirs)
        mine = None if lean else joint[0]
        pack, bias, vectors = call(
            functools.partial(level_vectors_kernel, k, k == 1),
            [f32(length(count_maps, high) + 8, 128), f32(2, 8, LANES), row],
            [VMEM] * 4,
        )(down, pack, vectors, others if k == 1 else theirs)
        downs.append(down)
        biases.append(bias)
        theirs = swap(pack, k + 1)
    hi, lo, add = call(
        functools.partial(paths_kernel, levels - 1),
        [jax.ShapeDtypeStruct((4, high, LANES), BF16)] * 2 + [f32(4, 8, LANES)],
        [VMEM] * (2 + len(downs) + len(biases)),
        flops=3000000000,
    )(*first_maps, *downs, *biases)
    keep, send = call(
        functools.partial(top_kernel, levels - 1), [f32(2, 8, LANES)] * 2, [VMEM] * 5
    )(vectors, theirs, hi, lo, add)
    theirs = swap(send, 0)
    own = call(own_kernel, [f32(cells, width)], [VMEM] * 5, flops=2000000000)(
        keep, inner, tail, half, ends
    )[0]
    return call(final_kernel, [f32(rows, cells, width)], [VMEM] * 6)(
        theirs, own, inner, tail, half, ends
    )[0]


def solution(mesh):
    return jax.shard_map(
        shards,
        mesh=mesh,
        in_specs=(
            P("surf", "line", None),
            P("surf", "line", None),
            P("surf", "line", None, None),
            P("surf", None),
            P("surf", "line", None, None),
            P("surf", "line", None, None),
            P("surf", "line", None, None),
        ),
        out_specs=P("surf", "line", None),
        check_vma=False,
    )
```

```python
import functools

import jax
import jax.numpy as jnp
from jax import lax
from jax.experimental import pallas as pl
from jax.experimental.pallas import tpu as pltpu
from jax.sharding import PartitionSpec as P

F32 = jnp.float32
BF16 = jnp.bfloat16
VMEM = pl.BlockSpec(memory_space=pltpu.VMEM)
LANES = 256
LIMIT = 12 * 1024 * 1024


def dot_nt(a, b):
    return lax.dot_general(a, b, (((1,), (1,)), ((), ())), preferred_element_type=F32)


def dot_nn(a, b):
    return lax.dot_general(a, b, (((1,), (0,)), ((), ())), preferred_element_type=F32)


def stacked(x):
    rest = x - x.astype(BF16).astype(F32)
    return jnp.concatenate([x, rest], axis=0).astype(BF16)


def times_block(x, block):
    n = x.shape[0]
    r = dot_nt(stacked(x), block)
    return r[:n] + r[n:]


def times_map(x, m):
    n = x.shape[0]
    hi = m.astype(BF16)
    lo = (m - hi.astype(F32)).astype(BF16)
    a = stacked(x)
    r = dot_nn(a, hi)
    return r[:n] + r[n:] + dot_nn(a[:n], lo)


def vector(row):
    return jnp.broadcast_to(row, (8, row.shape[1]))


def packed(maps):
    parts = [m[:, :128] for m in maps]
    parts += [jnp.transpose(m[:128, 128:])[:8] for m in maps]
    corner = maps[0][128:, 128:]
    for k, m in enumerate(maps[1:]):
        corner = corner + pltpu.roll(m[128:, 128:], 8 * k + 8, 1)
    return jnp.concatenate(parts + [corner], axis=0)


def length(count, high):
    return count * (high + 8) + 8


def unpacked(p, count, high):
    base = count * (high + 8)
    corner = p[base : base + 8]
    lane = lax.broadcasted_iota(jnp.int32, (8, 128), 1)
    maps = []
    for k in range(count):
        top = p[count * high + 8 * k : count * high + 8 * k + 8]
        top = jnp.transpose(jnp.concatenate([top, jnp.zeros((120, 128), F32)], axis=0))
        own = pltpu.roll(corner, 128 - 8 * k, 1) if k else corner
        right = jnp.concatenate([top, jnp.where(lane < 8, own, 0.0)], axis=0)
        maps.append(jnp.concatenate([p[k * high : k * high + high], right], axis=1))
    return maps


def unit_kernel(out):
    out[...] = (
        lax.broadcasted_iota(jnp.int32, out.shape, 0) == lax.broadcasted_iota(jnp.int32, out.shape, 1)
    ).astype(BF16)


def ready_kernel(unit, lower, upper, out):
    out[...] = unit[...]


def ahead_kernel(unit, lower, ahead):
    rows, cells, width, _ = lower.shape
    per = cells // 2
    eye = unit[...]
    now = {}
    for j in range(per):
        for l in range(rows):
            for p in range(2):
                block = lower[l, p * per + j]
                if j > 1:
                    now[l, p] = times_block(now[l, p], block)
                else:
                    now[l, p] = dot_nt(now[l, p].astype(BF16) if j else eye, block)
                ahead[l, p * per + j, :, :width] = now[l, p]


def maps_kernel(unit, ahead, upper, right, own, coupling, neighbours, tail, half, keep, send):
    rows, cells, width, _ = upper.shape
    high = keep.shape[1]
    per = cells // 2
    core = side(0)
    eye = unit[...]
    blank = jnp.zeros((high, LANES - 128), F32)
    for k in range(3):
        keep[k, :, 128:] = blank
        send[k, :, 128:] = blank
        for l in range(rows):
            half[l, k, :, 128:] = blank
    ends = [[ahead[l, p * per + per - 1, :, :width] for p in range(2)] for l in range(rows)]
    back = {}

    def step(l, p, j):
        i = p * per + j
        if j == per - 1:
            g, b = ends[l][p], dot_nt(eye, upper[l, i])
        elif j == per - 2:
            g, b = back[l, p]
            rest = g - g.astype(BF16).astype(F32)
            r = dot_nt(jnp.concatenate([g, rest, b], axis=0).astype(BF16), upper[l, i])
            g = ahead[l, i, :, :width] + (r[:high] + r[high : 2 * high])
            b = r[2 * high :]
        else:
            both = times_block(jnp.concatenate(back[l, p], axis=0), upper[l, i])
            g = ahead[l, i, :, :width] + both[:high]
            b = both[high:]
        back[l, p] = g, b
        tail[l, i, :high, :width] = g
        tail[l, i, high:, :width] = b

    for j in reversed(range(per)):
        for p in (1, 0):
            for l in range(rows):
                step(l, p, j)
        if j == per - 1:
            front = [times_map(f[0], f[1][:width]) for f in ends]
    joint = []
    for l in range(rows):
        g = back[l, 0][0], back[l, 1][0]
        b = back[l, 0][1], back[l, 1][1]
        inward = times_map(ends[l][0], g[1][:width])
        both = times_map(jnp.concatenate([inward, b[1]], axis=0), b[0][:width])
        for k, m in enumerate([ends[l][0], inward, ends[l][1]]):
            half[l, k, :, :width] = m
        joint.append([front[l], g[0] + both[:high], both[high:]])
    for k in range(3):
        keep[k, :, :width] = jnp.where(core == 0, joint[0][k], joint[1][k])
        send[k, :, :width] = jnp.where(core == 0, joint[1][k], joint[0][k])


def segment_kernel(
    patches, neighbours, right, own, first, second, coupling, pivots, lower, upper,
    tail, half, after, inner, bias, keep, send, pad,
):
    rows, cells, width = right.shape
    high = half.shape[2]
    per = cells // 2
    core = side(0)
    here = lax.axis_index("surf")
    odd = lax.rem(here, 2)
    after = lax.rem(here + 1, patches)
    before = lax.rem(here + patches - 1, patches)
    met = [here, jnp.where(odd == 0, after, before), jnp.where(odd == 0, before, after)]
    driven = []
    for l in range(rows):
        total = right[l]
        for f in range(coupling.shape[2]):
            line = jnp.broadcast_to(neighbours[l : l + 1, f : f + 1], (cells, width))
            near = jnp.zeros((cells, width), F32)
            for patch, held in zip(met, (own, first, second)):
                for r in range(rows):
                    near = jnp.where(line == patch * rows + r, held[r], near)
            total = total - coupling[l, :, f, :] * near
        driven.append(total)
    lhs = [stacked(d) for d in driven]
    chains = [(l, p) for l in range(rows) for p in range(2)]
    value, values, corr = {}, {}, {}
    for j in range(per):
        for l, p in chains:
            i = p * per + j
            r = dot_nt(lhs[l], pivots[l, i])
            d = vector(r[i : i + 1] + r[cells + i : cells + i + 1])
            if j:
                d = d + times_block(value[l, p], lower[l, i])
            value[l, p] = values[l, i] = d
    for j in reversed(range(per)):
        for l, p in chains:
            i = p * per + j
            d = values[l, i]
            if j < per - 1:
                d = d + times_block(corr[l, p], upper[l, i])
            corr[l, p] = d
            inner[l, i : i + 1, :] = d[:1]
    pad[...] = jnp.zeros(pad.shape, F32)
    ends = []
    for l in range(rows):
        for p in range(2):
            pad[l, p, :, :width] = value[l, p]
            pad[l, 2 + p, :, :width] = corr[l, p]
        f = [pad[l, 0], pad[l, 1]]
        g = [pad[l, 2], pad[l, 3]]
        v = merged_vectors(f, g, half[l, 2], tail[l, per, :high], tail[l, 0, high:])
        bias[l, 0] = f[0]
        bias[l, 1] = v[2]
        ends.append(v)
    keep[...] = jnp.zeros(keep.shape, F32)
    send[...] = jnp.zeros(send.shape, F32)
    for k in range(2):
        a, b = ends[0][k][:1, :width], ends[1][k][:1, :width]
        keep[k : k + 1, :width] = jnp.where(core == 0, a, b)
        send[k : k + 1, :width] = jnp.where(core == 0, b, a)


def side(level):
    return (lax.axis_index("line") >> level) & 1


def ordered(s, mine, theirs):
    return jnp.where(s == 0, mine, theirs), jnp.where(s == 0, theirs, mine)


def merged_maps(f, g, b):
    high = f[0].shape[0]
    lhs = f[0][:, :high]
    inward = times_map(lhs, g[1])
    both = times_map(jnp.concatenate([inward, b[1]], axis=0)[:, :high], b[0])
    return [times_map(lhs, f[1]), g[0] + both[:high], both[high:]], inward


def merged_vectors(f, g, f_right, g_right, b_left):
    high = f_right.shape[0]
    between = times_map(f[0][:, :high], g_right) + g[1]
    return times_map(f[0][:, :high], f_right) + f[1], g[0] + times_map(between[:, :high], b_left), between


def first_maps_kernel(mine, theirs, down, full, pack):
    s = side(0)
    f, g, b = (ordered(s, mine[k], theirs[k]) for k in range(3))
    joint, inward = merged_maps(f, g, b)
    down[...] = inward
    for k, m in enumerate(joint):
        full[k] = m
    pack[...] = packed(joint)


def first_vectors_kernel(maps, others, mine, theirs, out, bias):
    s = side(0)
    f = [vector(v) for v in ordered(s, mine[0:1], theirs[0:1])]
    g = [vector(v) for v in ordered(s, mine[1:2], theirs[1:2])]
    right = [jnp.where(s == 0, others[k], maps[k]) for k in range(2)]
    joint = merged_vectors(f, g, right[0], right[1], jnp.where(s == 0, maps[2], others[2]))
    out[...] = jnp.zeros(out.shape, F32)
    out[0:1] = joint[0][:1]
    out[1:2] = joint[1][:1]
    bias[0] = f[0]
    bias[1] = joint[2]


def level_maps_kernel(level, lean, mine, theirs, down, pack, full=None):
    high = mine.shape[1]
    maps = unpacked(theirs, 3, high)
    s = side(level)
    f, g, b = (ordered(s, mine[k], maps[k]) for k in range(3))
    lhs = f[0][:, :high]
    if lean:
        through = times_map(g[1][:, :high], b[0])
        joint = [g[0] + times_map(lhs, through)]
    else:
        both = times_map(jnp.concatenate([g[1], b[1]], axis=0)[:, :high], b[0])
        through = both[:high]
        joint = [times_map(lhs, f[1]), g[0] + times_map(lhs, through), both[high:]]
    pack[...] = packed(joint)
    for k, m in enumerate([f[0], b[1], f[1], g[1], b[0], through]):
        down[k] = m
    for k, m in enumerate(joint if not lean else []):
        full[k] = m


def level_vectors_kernel(level, split, down, pack, vectors, theirs, out, bias, ends):
    s = side(level)
    base = pack.shape[0]
    other = [theirs[0:1], theirs[1:2]] if split else tail_vectors(theirs, theirs.shape[0] - 8)
    vf = [vector(v) for v in ordered(s, vectors[0:1], other[0])]
    vg = [vector(v) for v in ordered(s, vectors[1:2], other[1])]
    high = down.shape[1]
    lhs = vf[0][:, :high]
    v = (
        times_map(lhs, down[2]) + vf[1],
        vg[0] + times_map(lhs, down[5]) + times_map(vg[1][:, :high], down[4]),
        times_map(lhs, down[3]) + vg[1],
    )
    bias[0] = vf[0]
    bias[1] = v[2]
    both = jnp.concatenate([v[0][:1], v[1][:1]], axis=0)
    out[:base] = pack[...]
    out[base : base + 2] = both[:, :128]
    out[base + 2 : base + 4] = both[:, 128:]
    out[base + 4 : base + 8] = jnp.zeros((4, 128), F32)
    ends[0:2] = both


def tail_vectors(theirs, base):
    return [
        jnp.concatenate([theirs[base + k : base + k + 1], theirs[base + 2 + k : base + 3 + k]], axis=1)
        for k in range(2)
    ]


def paths_kernel(levels, *refs):
    maps, others, first_inward = refs[:3]
    downs, biases = refs[3 : levels + 2], refs[levels + 2 : 2 * levels + 2]
    hi, lo, add = refs[-3:]
    high = maps.shape[1]
    top = side(levels) == 1
    s = side(0)
    eye = (
        lax.broadcasted_iota(jnp.int32, (high, LANES), 0)
        == lax.broadcasted_iota(jnp.int32, (high, LANES), 1)
    ).astype(F32)
    nothing = jnp.zeros((8, LANES), F32)
    value = jnp.concatenate([jnp.where(top, eye, 0.0), nothing], axis=0)
    corr = jnp.concatenate([jnp.where(top, 0.0, eye), nothing], axis=0)
    for k in reversed(range(levels)):
        if k:
            d = downs[k - 1]
            f, b = d[0], d[1]
            inward = times_map(f[:, :high], d[3])
        else:
            f = jnp.where(s == 0, maps[0], others[0])
            b = jnp.where(s == 0, others[2], maps[2])
            inward = first_inward[...]
        if k == levels - 1:
            middle, back = jnp.where(top, f, 0.0), jnp.where(top, inward, b)
            middle = jnp.concatenate([middle, nothing], axis=0)
            back = jnp.concatenate([back, nothing], axis=0)
        else:
            lhs = value[:, :high]
            middle = times_map(lhs, f)
            back = times_map(lhs, inward) + times_map(corr[:, :high], b)
        base = jnp.zeros((high, LANES), F32)
        middle = middle + jnp.concatenate([base, biases[k][0]], axis=0)
        back = back + jnp.concatenate([base, biases[k][1]], axis=0)
        if k:
            value = jnp.where(side(k) == 0, value, middle)
            corr = jnp.where(side(k) == 0, back, corr)
    paths = [
        jnp.where(s == 0, value, middle), jnp.where(s == 0, back, corr),
        jnp.where(s == 0, middle, value), jnp.where(s == 0, corr, back),
    ]
    for k, m in enumerate(paths):
        top_term = m[:high].astype(BF16)
        hi[k] = top_term
        lo[k] = (m[:high] - top_term.astype(F32)).astype(BF16)
        add[k] = m[high:]


def top_kernel(level, vectors, theirs, hi, lo, add, keep, send):
    high = hi.shape[1]
    g = unpacked(theirs, 1, high)[0]
    other = [vector(v) for v in tail_vectors(theirs, length(1, high))]
    ours = vector(vectors[0:1])
    back = times_map(ours[:, :high], g) + other[1]
    x = jnp.where(side(level) == 0, back, other[0])[:, :high]
    a = stacked(x)
    for k in range(4):
        r = dot_nn(a, hi[k])
        r = r[:8] + r[8:] + dot_nn(a[:8], lo[k]) + add[k]
        if k < 2:
            keep[k] = r
        else:
            send[k - 2] = r


def solved(line, ends, inner, tail, half, bias):
    _, cells, width = inner.shape
    high = half.shape[2]
    per = cells // 2
    y, c = ends[0], ends[1]
    lhs = y[:, :high]
    middle = times_map(lhs, half[line, 0]) + bias[line, 0]
    between = (
        times_map(lhs, half[line, 1])
        + times_map(c[:, :high], tail[line, per, high:])
        + bias[line, 1]
    )
    index = lax.broadcasted_iota(jnp.int32, (8, LANES), 0)
    gathered = jnp.zeros((8, LANES), F32)
    for k, v in enumerate([y, between, middle, c]):
        gathered = jnp.where(index == k, v, gathered)
    columns = jnp.transpose(gathered)[:high]
    columns = [jnp.broadcast_to(columns[:, k : k + 1], (high, 128)) for k in range(4)]
    parts = []
    for h in range(2):
        at = slice(128 * h, min(width, 128 * h + 128))
        sums = []
        for i in range(cells):
            k = 2 * (i // per)
            t = (
                tail[line, i, :high, 128 * h : 128 * h + 128] * columns[k]
                + tail[line, i, high:, 128 * h : 128 * h + 128] * columns[k + 1]
            )
            sums.append(jnp.sum(t, axis=0, keepdims=True)[:, : at.stop - at.start])
        parts.append((at, jnp.concatenate(sums, axis=0) + inner[line, :, at]))
    return parts


def own_kernel(ends, inner, tail, half, bias, out):
    for at, value in solved(side(0), ends, inner, tail, half, bias):
        out[:, at] = value


def final_kernel(ends, own, inner, tail, half, bias, out):
    core = side(0)
    other = 1 - core
    out[core] = own[...]
    for at, value in solved(other, ends, inner, tail, half, bias):
        out[other, :, at] = value


def call(body, outs, specs, scratch=(), flops=None):
    return pl.pallas_call(
        body,
        out_shape=outs,
        in_specs=specs,
        out_specs=jax.tree.map(lambda _: VMEM, outs),
        scratch_shapes=scratch,
        cost_estimate=flops and pl.CostEstimate(flops=flops, bytes_accessed=0, transcendentals=0),
        compiler_params=pltpu.CompilerParams(vmem_limit_bytes=LIMIT),
    )


def f32(*shape):
    return jax.ShapeDtypeStruct(shape, F32)


def shards(right_side, previous, coupling, neighbours, pivots, lower_factor, upper_factor):
    rows, cells, width = right_side.shape
    high = width + 1
    patches = lax.axis_size("surf")
    count = lax.axis_size("line")
    levels = count.bit_length() - 1
    pairs = [(i, i + 1 - 2 * (i % 2)) for i in range(patches)]
    odd = [(i, (i - 1 + 2 * (i % 2)) % patches) for i in range(patches)]
    swap = lambda a, k: lax.ppermute(a, "line", [(i, i ^ (1 << k)) for i in range(count)])
    second = lax.ppermute(previous, "surf", odd)
    first = lax.ppermute(previous, "surf", pairs)
    full = f32(3, high, LANES)
    row = f32(8, LANES)
    unit = call(unit_kernel, [jax.ShapeDtypeStruct((high, width), BF16)], [], flops=2000000000)()[0]
    unit = call(ready_kernel, [jax.ShapeDtypeStruct((high, width), BF16)], [VMEM] * 3)(
        unit, jnp.transpose(lower_factor, (0, 2, 1, 3)), jnp.transpose(upper_factor, (0, 2, 1, 3))
    )[0]
    unit, lower_factor, upper_factor = lax.optimization_barrier(
        (unit, lower_factor, upper_factor)
    )
    ahead = call(ahead_kernel, [f32(rows, cells, high, LANES)], [VMEM] * 2, flops=12000000000)(
        unit, lower_factor
    )[0]
    tail, half, keep, send = call(
        maps_kernel,
        [f32(rows, cells, 2 * high, LANES), f32(rows, 3, high, LANES), full, full],
        [VMEM] * 7,
        flops=12000000000,
    )(unit, ahead, upper_factor, right_side, previous, coupling, neighbours)
    send, first = lax.optimization_barrier((send, first))
    theirs = swap(send, 0)
    first_maps = keep, theirs
    down, mine, pack = call(
        first_maps_kernel,
        [f32(high, LANES), full, f32(length(3, high), 128)],
        [VMEM] * 2,
    )(keep, theirs)
    theirs = swap(pack, 1)
    pack, pivots = lax.optimization_barrier((pack, pivots))
    inner, ends, vkeep, vsend = call(
        functools.partial(segment_kernel, patches),
        [f32(rows, cells, width), f32(rows, 2, 8, LANES), row, row],
        [VMEM] * 12,
        [pltpu.VMEM((rows, 4, 8, LANES), F32)],
        50000000000,
    )(
        neighbours, right_side, previous, first, second, coupling, pivots,
        lower_factor, upper_factor, tail, half, pack,
    )
    vtheirs = swap(vsend, 0)
    vectors, bias = call(
        first_vectors_kernel, [row, f32(2, 8, LANES)], [VMEM] * 4
    )(*first_maps, vkeep, vtheirs)
    others = swap(vectors, 1)
    downs = [down]
    biases = [bias]
    for k in range(1, levels - 1):
        lean = k == levels - 2
        count_maps = 1 if lean else 3
        down, pack, *joint = call(
            functools.partial(level_maps_kernel, k, lean),
            [
                f32(6, high, LANES), f32(length(count_maps, high), 128),
            ] + ([] if lean else [full]),
            [VMEM] * 2,
            flops=20000000000,
        )(mine, theirs)
        mine = None if lean else joint[0]
        pack, bias, vectors = call(
            functools.partial(level_vectors_kernel, k, k == 1),
            [f32(length(count_maps, high) + 8, 128), f32(2, 8, LANES), row],
            [VMEM] * 4,
        )(down, pack, vectors, others if k == 1 else theirs)
        downs.append(down)
        biases.append(bias)
        theirs = swap(pack, k + 1)
    hi, lo, add = call(
        functools.partial(paths_kernel, levels - 1),
        [jax.ShapeDtypeStruct((4, high, LANES), BF16)] * 2 + [f32(4, 8, LANES)],
        [VMEM] * (2 + len(downs) + len(biases)),
        flops=3000000000,
    )(*first_maps, *downs, *biases)
    keep, send = call(
        functools.partial(top_kernel, levels - 1), [f32(2, 8, LANES)] * 2, [VMEM] * 5
    )(vectors, theirs, hi, lo, add)
    theirs = swap(send, 0)
    own = call(own_kernel, [f32(cells, width)], [VMEM] * 5, flops=2000000000)(
        keep, inner, tail, half, ends
    )[0]
    return call(final_kernel, [f32(rows, cells, width)], [VMEM] * 6)(
        theirs, own, inner, tail, half, ends
    )[0]


def solution(mesh):
    return jax.shard_map(
        shards,
        mesh=mesh,
        in_specs=(
            P("surf", "line", None),
            P("surf", "line", None),
            P("surf", "line", None, None),
            P("surf", None),
            P("surf", "line", None, None),
            P("surf", "line", None, None),
            P("surf", "line", None, None),
        ),
        out_specs=P("surf", "line", None),
        check_vma=False,
    )
```

```python
import functools

import jax
import jax.numpy as jnp
from jax import lax
from jax.experimental import pallas as pl
from jax.experimental.pallas import tpu as pltpu
from jax.sharding import PartitionSpec as P

F32 = jnp.float32
BF16 = jnp.bfloat16
VMEM = pl.BlockSpec(memory_space=pltpu.VMEM)
LANES = 256
LIMIT = 12 * 1024 * 1024


def dot_nt(a, b):
    return lax.dot_general(a, b, (((1,), (1,)), ((), ())), preferred_element_type=F32)


def dot_nn(a, b):
    return lax.dot_general(a, b, (((1,), (0,)), ((), ())), preferred_element_type=F32)


def stacked(x):
    rest = x - x.astype(BF16).astype(F32)
    return jnp.concatenate([x, rest], axis=0).astype(BF16)


def times_block(x, block):
    n = x.shape[0]
    r = dot_nt(stacked(x), block)
    return r[:n] + r[n:]


def times_map(x, m):
    n = x.shape[0]
    hi = m.astype(BF16)
    lo = (m - hi.astype(F32)).astype(BF16)
    a = stacked(x)
    r = dot_nn(a, hi)
    return r[:n] + r[n:] + dot_nn(a[:n], lo)


def vector(row):
    return jnp.broadcast_to(row, (8, row.shape[1]))


def packed(maps):
    parts = [m[:, :128] for m in maps]
    parts += [jnp.transpose(m[:128, 128:])[:8] for m in maps]
    corner = maps[0][128:, 128:]
    for k, m in enumerate(maps[1:]):
        corner = corner + pltpu.roll(m[128:, 128:], 8 * k + 8, 1)
    return jnp.concatenate(parts + [corner], axis=0)


def length(count, high):
    return count * (high + 8) + 8


def unpacked(p, count, high):
    base = count * (high + 8)
    corner = p[base : base + 8]
    lane = lax.broadcasted_iota(jnp.int32, (8, 128), 1)
    maps = []
    for k in range(count):
        top = p[count * high + 8 * k : count * high + 8 * k + 8]
        top = jnp.transpose(jnp.concatenate([top, jnp.zeros((120, 128), F32)], axis=0))
        own = pltpu.roll(corner, 128 - 8 * k, 1) if k else corner
        right = jnp.concatenate([top, jnp.where(lane < 8, own, 0.0)], axis=0)
        maps.append(jnp.concatenate([p[k * high : k * high + high], right], axis=1))
    return maps


def unit_kernel(out):
    out[...] = (
        lax.broadcasted_iota(jnp.int32, out.shape, 0) == lax.broadcasted_iota(jnp.int32, out.shape, 1)
    ).astype(BF16)


def ready_kernel(unit, lower, upper, out):
    out[...] = unit[...]


def ahead_kernel(unit, lower, ahead):
    rows, cells, width, _ = lower.shape
    per = cells // 2
    eye = unit[...]
    now = {}
    for j in range(per):
        for l in range(rows):
            for p in range(2):
                block = lower[l, p * per + j]
                if j > 1:
                    now[l, p] = times_block(now[l, p], block)
                else:
                    now[l, p] = dot_nt(now[l, p].astype(BF16) if j else eye, block)
                ahead[l, p * per + j, :, :width] = now[l, p]


def maps_kernel(unit, ahead, upper, tail, half, keep, send, spare):
    rows, cells, width, _ = upper.shape
    high = keep.shape[1]
    per = cells // 2
    core = side(0)
    eye = unit[...]
    blank = jnp.zeros((high, LANES - 128), F32)
    for k in range(3):
        keep[k, :, 128:] = blank
        spare[k, :, 128:] = blank
        for l in range(rows):
            half[l, k, :, 128:] = blank
    ends = [[ahead[l, p * per + per - 1, :, :width] for p in range(2)] for l in range(rows)]
    back = {}

    def step(l, p, j):
        i = p * per + j
        if j == per - 1:
            g, b = ends[l][p], dot_nt(eye, upper[l, i])
        elif j == per - 2:
            g, b = back[l, p]
            rest = g - g.astype(BF16).astype(F32)
            r = dot_nt(jnp.concatenate([g, rest, b], axis=0).astype(BF16), upper[l, i])
            g = ahead[l, i, :, :width] + (r[:high] + r[high : 2 * high])
            b = r[2 * high :]
        else:
            both = times_block(jnp.concatenate(back[l, p], axis=0), upper[l, i])
            g = ahead[l, i, :, :width] + both[:high]
            b = both[high:]
        back[l, p] = g, b
        tail[l, i, :high, :width] = g
        tail[l, i, high:, :width] = b

    for j in reversed(range(per)):
        for p in (1, 0):
            for l in range(rows):
                step(l, p, j)
        if j == per - 1:
            front = [times_map(f[0], f[1][:width]) for f in ends]
    joint = []
    for l in range(rows):
        g = back[l, 0][0], back[l, 1][0]
        b = back[l, 0][1], back[l, 1][1]
        inward = times_map(ends[l][0], g[1][:width])
        both = times_map(jnp.concatenate([inward, b[1]], axis=0), b[0][:width])
        for k, m in enumerate([ends[l][0], inward, ends[l][1]]):
            half[l, k, :, :width] = m
        joint.append([front[l], g[0] + both[:high], both[high:]])
    for k in range(3):
        keep[k, :, :width] = jnp.where(core == 0, joint[0][k], joint[1][k])
        spare[k, :, :width] = jnp.where(core == 0, joint[1][k], joint[0][k])
    send[...] = packed([spare[k] for k in range(3)])


def segment_kernel(
    patches, neighbours, right, own, first, second, coupling, pivots, lower, upper,
    tail, half, after, inner, bias, keep, send, pad,
):
    rows, cells, width = right.shape
    high = half.shape[2]
    per = cells // 2
    core = side(0)
    here = lax.axis_index("surf")
    odd = lax.rem(here, 2)
    after = lax.rem(here + 1, patches)
    before = lax.rem(here + patches - 1, patches)
    met = [here, jnp.where(odd == 0, after, before), jnp.where(odd == 0, before, after)]
    driven = []
    for l in range(rows):
        total = right[l]
        for f in range(coupling.shape[2]):
            line = jnp.broadcast_to(neighbours[l : l + 1, f : f + 1], (cells, width))
            near = jnp.zeros((cells, width), F32)
            for patch, held in zip(met, (own, first, second)):
                for r in range(rows):
                    near = jnp.where(line == patch * rows + r, held[r], near)
            total = total - coupling[l, :, f, :] * near
        driven.append(total)
    lhs = [stacked(d) for d in driven]
    chains = [(l, p) for l in range(rows) for p in range(2)]
    value, values, corr = {}, {}, {}
    for j in range(per):
        for l, p in chains:
            i = p * per + j
            r = dot_nt(lhs[l], pivots[l, i])
            d = vector(r[i : i + 1] + r[cells + i : cells + i + 1])
            if j:
                d = d + times_block(value[l, p], lower[l, i])
            value[l, p] = values[l, i] = d
    for j in reversed(range(per)):
        for l, p in chains:
            i = p * per + j
            d = values[l, i]
            if j < per - 1:
                d = d + times_block(corr[l, p], upper[l, i])
            corr[l, p] = d
            inner[l, i : i + 1, :] = d[:1]
    pad[...] = jnp.zeros(pad.shape, F32)
    ends = []
    for l in range(rows):
        for p in range(2):
            pad[l, p, :, :width] = value[l, p]
            pad[l, 2 + p, :, :width] = corr[l, p]
        f = [pad[l, 0], pad[l, 1]]
        g = [pad[l, 2], pad[l, 3]]
        v = merged_vectors(f, g, half[l, 2], tail[l, per, :high], tail[l, 0, high:])
        bias[l, 0] = f[0]
        bias[l, 1] = v[2]
        ends.append(v)
    keep[...] = jnp.zeros(keep.shape, F32)
    send[...] = jnp.zeros(send.shape, F32)
    for k in range(2):
        a, b = ends[0][k][:1, :width], ends[1][k][:1, :width]
        keep[k : k + 1, :width] = jnp.where(core == 0, a, b)
        send[k : k + 1, :width] = jnp.where(core == 0, b, a)


def side(level):
    return (lax.axis_index("line") >> level) & 1


def ordered(s, mine, theirs):
    return jnp.where(s == 0, mine, theirs), jnp.where(s == 0, theirs, mine)


def merged_maps(f, g, b):
    high = f[0].shape[0]
    lhs = f[0][:, :high]
    inward = times_map(lhs, g[1])
    both = times_map(jnp.concatenate([inward, b[1]], axis=0)[:, :high], b[0])
    return [times_map(lhs, f[1]), g[0] + both[:high], both[high:]], inward


def merged_vectors(f, g, f_right, g_right, b_left):
    high = f_right.shape[0]
    between = times_map(f[0][:, :high], g_right) + g[1]
    return times_map(f[0][:, :high], f_right) + f[1], g[0] + times_map(between[:, :high], b_left), between


def first_maps_kernel(mine, theirs, down, other, full, pack):
    s = side(0)
    maps = unpacked(theirs, 3, mine.shape[1])
    for k in range(3):
        other[k] = maps[k]
    f, g, b = (ordered(s, mine[k], maps[k]) for k in range(3))
    joint, inward = merged_maps(f, g, b)
    down[...] = inward
    for k, m in enumerate(joint):
        full[k] = m
    pack[...] = packed(joint)


def first_vectors_kernel(maps, others, mine, theirs, out, bias):
    s = side(0)
    f = [vector(v) for v in ordered(s, mine[0:1], theirs[0:1])]
    g = [vector(v) for v in ordered(s, mine[1:2], theirs[1:2])]
    right = [jnp.where(s == 0, others[k], maps[k]) for k in range(2)]
    joint = merged_vectors(f, g, right[0], right[1], jnp.where(s == 0, maps[2], others[2]))
    out[...] = jnp.zeros(out.shape, F32)
    out[0:1] = joint[0][:1]
    out[1:2] = joint[1][:1]
    bias[0] = f[0]
    bias[1] = joint[2]


def level_maps_kernel(level, lean, mine, theirs, down, pack, full=None):
    high = mine.shape[1]
    maps = unpacked(theirs, 3, high)
    s = side(level)
    f, g, b = (ordered(s, mine[k], maps[k]) for k in range(3))
    lhs = f[0][:, :high]
    if lean:
        through = times_map(g[1][:, :high], b[0])
        joint = [g[0] + times_map(lhs, through)]
    else:
        both = times_map(jnp.concatenate([g[1], b[1]], axis=0)[:, :high], b[0])
        through = both[:high]
        joint = [times_map(lhs, f[1]), g[0] + times_map(lhs, through), both[high:]]
    pack[...] = packed(joint)
    for k, m in enumerate([f[0], b[1], f[1], g[1], b[0], through]):
        down[k] = m
    for k, m in enumerate(joint if not lean else []):
        full[k] = m


def level_vectors_kernel(level, split, down, pack, vectors, theirs, out, bias, ends):
    s = side(level)
    base = pack.shape[0]
    other = [theirs[0:1], theirs[1:2]] if split else tail_vectors(theirs, theirs.shape[0] - 8)
    vf = [vector(v) for v in ordered(s, vectors[0:1], other[0])]
    vg = [vector(v) for v in ordered(s, vectors[1:2], other[1])]
    high = down.shape[1]
    lhs = vf[0][:, :high]
    v = (
        times_map(lhs, down[2]) + vf[1],
        vg[0] + times_map(lhs, down[5]) + times_map(vg[1][:, :high], down[4]),
        times_map(lhs, down[3]) + vg[1],
    )
    bias[0] = vf[0]
    bias[1] = v[2]
    both = jnp.concatenate([v[0][:1], v[1][:1]], axis=0)
    out[:base] = pack[...]
    out[base : base + 2] = both[:, :128]
    out[base + 2 : base + 4] = both[:, 128:]
    out[base + 4 : base + 8] = jnp.zeros((4, 128), F32)
    ends[0:2] = both


def tail_vectors(theirs, base):
    return [
        jnp.concatenate([theirs[base + k : base + k + 1], theirs[base + 2 + k : base + 3 + k]], axis=1)
        for k in range(2)
    ]


def paths_kernel(levels, *refs):
    maps, others, first_inward = refs[:3]
    downs, biases = refs[3 : levels + 2], refs[levels + 2 : 2 * levels + 2]
    hi, lo, add = refs[-3:]
    high = maps.shape[1]
    top = side(levels) == 1
    s = side(0)
    eye = (
        lax.broadcasted_iota(jnp.int32, (high, LANES), 0)
        == lax.broadcasted_iota(jnp.int32, (high, LANES), 1)
    ).astype(F32)
    nothing = jnp.zeros((8, LANES), F32)
    value = jnp.concatenate([jnp.where(top, eye, 0.0), nothing], axis=0)
    corr = jnp.concatenate([jnp.where(top, 0.0, eye), nothing], axis=0)
    for k in reversed(range(levels)):
        if k:
            d = downs[k - 1]
            f, b = d[0], d[1]
            inward = times_map(f[:, :high], d[3])
        else:
            f = jnp.where(s == 0, maps[0], others[0])
            b = jnp.where(s == 0, others[2], maps[2])
            inward = first_inward[...]
        if k == levels - 1:
            middle, back = jnp.where(top, f, 0.0), jnp.where(top, inward, b)
            middle = jnp.concatenate([middle, nothing], axis=0)
            back = jnp.concatenate([back, nothing], axis=0)
        else:
            lhs = value[:, :high]
            middle = times_map(lhs, f)
            back = times_map(lhs, inward) + times_map(corr[:, :high], b)
        base = jnp.zeros((high, LANES), F32)
        middle = middle + jnp.concatenate([base, biases[k][0]], axis=0)
        back = back + jnp.concatenate([base, biases[k][1]], axis=0)
        if k:
            value = jnp.where(side(k) == 0, value, middle)
            corr = jnp.where(side(k) == 0, back, corr)
    paths = [
        jnp.where(s == 0, value, middle), jnp.where(s == 0, back, corr),
        jnp.where(s == 0, middle, value), jnp.where(s == 0, corr, back),
    ]
    for k, m in enumerate(paths):
        top_term = m[:high].astype(BF16)
        hi[k] = top_term
        lo[k] = (m[:high] - top_term.astype(F32)).astype(BF16)
        add[k] = m[high:]


def top_kernel(level, vectors, theirs, hi, lo, add, keep, send):
    high = hi.shape[1]
    g = unpacked(theirs, 1, high)[0]
    other = [vector(v) for v in tail_vectors(theirs, length(1, high))]
    ours = vector(vectors[0:1])
    back = times_map(ours[:, :high], g) + other[1]
    x = jnp.where(side(level) == 0, back, other[0])[:, :high]
    a = stacked(x)
    for k in range(4):
        r = dot_nn(a, hi[k])
        r = r[:8] + r[8:] + dot_nn(a[:8], lo[k]) + add[k]
        if k < 2:
            keep[k] = r
        else:
            send[k - 2] = r


def solved(line, ends, inner, tail, half, bias):
    _, cells, width = inner.shape
    high = half.shape[2]
    per = cells // 2
    y, c = ends[0], ends[1]
    lhs = y[:, :high]
    middle = times_map(lhs, half[line, 0]) + bias[line, 0]
    between = (
        times_map(lhs, half[line, 1])
        + times_map(c[:, :high], tail[line, per, high:])
        + bias[line, 1]
    )
    index = lax.broadcasted_iota(jnp.int32, (8, LANES), 0)
    gathered = jnp.zeros((8, LANES), F32)
    for k, v in enumerate([y, between, middle, c]):
        gathered = jnp.where(index == k, v, gathered)
    columns = jnp.transpose(gathered)[:high]
    columns = [jnp.broadcast_to(columns[:, k : k + 1], (high, 128)) for k in range(4)]
    parts = []
    for h in range(2):
        at = slice(128 * h, min(width, 128 * h + 128))
        sums = []
        for i in range(cells):
            k = 2 * (i // per)
            t = (
                tail[line, i, :high, 128 * h : 128 * h + 128] * columns[k]
                + tail[line, i, high:, 128 * h : 128 * h + 128] * columns[k + 1]
            )
            sums.append(jnp.sum(t, axis=0, keepdims=True)[:, : at.stop - at.start])
        parts.append((at, jnp.concatenate(sums, axis=0) + inner[line, :, at]))
    return parts


def own_kernel(ends, inner, tail, half, bias, out):
    for at, value in solved(side(0), ends, inner, tail, half, bias):
        out[:, at] = value


def final_kernel(ends, own, inner, tail, half, bias, out):
    core = side(0)
    other = 1 - core
    out[core] = own[...]
    for at, value in solved(other, ends, inner, tail, half, bias):
        out[other, :, at] = value


def call(body, outs, specs, scratch=(), flops=None):
    return pl.pallas_call(
        body,
        out_shape=outs,
        in_specs=specs,
        out_specs=jax.tree.map(lambda _: VMEM, outs),
        scratch_shapes=scratch,
        cost_estimate=flops and pl.CostEstimate(flops=flops, bytes_accessed=0, transcendentals=0),
        compiler_params=pltpu.CompilerParams(vmem_limit_bytes=LIMIT),
    )


def f32(*shape):
    return jax.ShapeDtypeStruct(shape, F32)


def shards(right_side, previous, coupling, neighbours, pivots, lower_factor, upper_factor):
    rows, cells, width = right_side.shape
    high = width + 1
    patches = lax.axis_size("surf")
    count = lax.axis_size("line")
    levels = count.bit_length() - 1
    pairs = [(i, i + 1 - 2 * (i % 2)) for i in range(patches)]
    odd = [(i, (i - 1 + 2 * (i % 2)) % patches) for i in range(patches)]
    swap = lambda a, k: lax.ppermute(a, "line", [(i, i ^ (1 << k)) for i in range(count)])
    second = lax.ppermute(previous, "surf", odd)
    first = lax.ppermute(previous, "surf", pairs)
    full = f32(3, high, LANES)
    row = f32(8, LANES)
    unit = call(unit_kernel, [jax.ShapeDtypeStruct((high, width), BF16)], [], flops=2000000000)()[0]
    unit = call(ready_kernel, [jax.ShapeDtypeStruct((high, width), BF16)], [VMEM] * 3)(
        unit, jnp.transpose(lower_factor, (0, 2, 1, 3)), jnp.transpose(upper_factor, (0, 2, 1, 3))
    )[0]
    unit, lower_factor, upper_factor = lax.optimization_barrier(
        (unit, lower_factor, upper_factor)
    )
    ahead = call(ahead_kernel, [f32(rows, cells, high, LANES)], [VMEM] * 2, flops=12000000000)(
        unit, lower_factor
    )[0]
    tail, half, keep, send = call(
        maps_kernel,
        [
            f32(rows, cells, 2 * high, LANES), f32(rows, 3, high, LANES), full,
            f32(length(3, high), 128),
        ],
        [VMEM] * 3,
        [pltpu.VMEM((3, high, LANES), F32)],
        flops=12000000000,
    )(unit, ahead, upper_factor)
    send, second, pivots = lax.optimization_barrier((send, second, pivots))
    theirs = swap(send, 0)
    down, theirs, mine, pack = call(
        first_maps_kernel,
        [f32(high, LANES), full, full, f32(length(3, high), 128)],
        [VMEM] * 2,
    )(keep, theirs)
    first_maps = keep, theirs
    theirs = swap(pack, 1)
    inner, ends, vkeep, vsend = call(
        functools.partial(segment_kernel, patches),
        [f32(rows, cells, width), f32(rows, 2, 8, LANES), row, row],
        [VMEM] * 12,
        [pltpu.VMEM((rows, 4, 8, LANES), F32)],
        50000000000,
    )(
        neighbours, right_side, previous, first, second, coupling, pivots,
        lower_factor, upper_factor, tail, half, pack,
    )
    vtheirs = swap(vsend, 0)
    vectors, bias = call(
        first_vectors_kernel, [row, f32(2, 8, LANES)], [VMEM] * 4
    )(*first_maps, vkeep, vtheirs)
    others = swap(vectors, 1)
    downs = [down]
    biases = [bias]
    for k in range(1, levels - 1):
        lean = k == levels - 2
        count_maps = 1 if lean else 3
        down, pack, *joint = call(
            functools.partial(level_maps_kernel, k, lean),
            [
                f32(6, high, LANES), f32(length(count_maps, high), 128),
            ] + ([] if lean else [full]),
            [VMEM] * 2,
            flops=20000000000,
        )(mine, theirs)
        mine = None if lean else joint[0]
        pack, bias, vectors = call(
            functools.partial(level_vectors_kernel, k, k == 1),
            [f32(length(count_maps, high) + 8, 128), f32(2, 8, LANES), row],
            [VMEM] * 4,
        )(down, pack, vectors, others if k == 1 else theirs)
        downs.append(down)
        biases.append(bias)
        theirs = swap(pack, k + 1)
    hi, lo, add = call(
        functools.partial(paths_kernel, levels - 1),
        [jax.ShapeDtypeStruct((4, high, LANES), BF16)] * 2 + [f32(4, 8, LANES)],
        [VMEM] * (2 + len(downs) + len(biases)),
        flops=3000000000,
    )(*first_maps, *downs, *biases)
    keep, send = call(
        functools.partial(top_kernel, levels - 1), [f32(2, 8, LANES)] * 2, [VMEM] * 5
    )(vectors, theirs, hi, lo, add)
    theirs = swap(send, 0)
    own = call(own_kernel, [f32(cells, width)], [VMEM] * 5, flops=2000000000)(
        keep, inner, tail, half, ends
    )[0]
    return call(final_kernel, [f32(rows, cells, width)], [VMEM] * 6)(
        theirs, own, inner, tail, half, ends
    )[0]


def solution(mesh):
    return jax.shard_map(
        shards,
        mesh=mesh,
        in_specs=(
            P("surf", "line", None),
            P("surf", "line", None),
            P("surf", "line", None, None),
            P("surf", None),
            P("surf", "line", None, None),
            P("surf", "line", None, None),
            P("surf", "line", None, None),
        ),
        out_specs=P("surf", "line", None),
        check_vma=False,
    )
```
